32 devices in a mesh: ray: 8 (over z, x), row: 4 (over y, core).
Axes of the slice: x: 2, y: 2, z: 4, core: 2. Of those that a mesh axis runs over, the one named last changes fastest.
Arguments:
- density: float32 [256, 64, 1024], P('ray', 'row'), may hold values from 0.2 to 5
- light_dir: float32 [3], replicated, may hold values from -1 to 1
- colour_tint: float32 [3], replicated, may hold values from 0.5 to 2
- cotangent: float32 [3, 64, 1024], P(None, 'row'), may hold values from -6 to 6
Outputs:
- dens_grad: float32 [256, 64, 1024], P('ray', 'row')
The draws below stay inside these ranges and needn't reach their ends.
All inputs are finite; a program needn't handle non-finite values.
Results may differ from the reference program's by a relative error of at most 0.0003.
Values sent between devices are 32-bit elements; how exact they have to be, the bound alone decides.
A program may use at most 128 MiB of HBM per device.

```python
import math
import jax
import jax.numpy as jnp
from jax import lax

NCOL = 1024
NDEP = 256
NROW = 64


def steps_of(rng, dims, cuts, least, largest):
    loudness = 1.0
    for axis_at, shards_of in cuts:
        steps = jax.random.uniform(jax.random.fold_in(jax.random.fold_in(rng, 6), axis_at), (shards_of,), jnp.float32, least / len(cuts), largest / len(cuts))
        loudness = loudness * jnp.repeat(jnp.exp(steps), dims[axis_at] // shards_of).reshape((-1,) + (1,) * (len(dims) - 1 - axis_at))
    return loudness


def bell_draw(key, dims, width, limit, split=(), kind=jnp.bfloat16):
    values = jax.random.normal(key, dims, jnp.float32) * width
    if len(split) > 0:
        values = steps_of(key, dims, split, -0.22, 0.18) * values
    return jnp.clip(values, min=-limit, max=limit).astype(kind)


def setup_inputs(seed: int = 0) -> dict:
    key_list = jax.random.split(jax.random.key(seed), 5)
    density = jnp.clip(jnp.exp(math.log(5.0) - 3.218876 * jax.random.uniform(key_list[0], (NDEP, NROW, NCOL), jnp.float32) ** steps_of(key_list[0], (NDEP, NROW, NCOL), ((0, 8), (1, 4)), -0.2, 0.2)), 0.2, 5.0)
    light_dir = jnp.clip(jax.random.uniform(key_list[1], (3,), jnp.float32, -1.0, 1.0), -1.0, 1.0)
    colour_tint = jnp.clip(jnp.exp(jax.random.uniform(key_list[2], (3,), jnp.float32, math.log(0.5), math.log(2.0))), 0.5, 2.0)
    cotangent = bell_draw(key_list[3], (3, NROW, NCOL), 1.0, 6.0, ((1, 4),), jnp.float32)
    return {"density": density, "light_dir": light_dir, "colour_tint": colour_tint, "cotangent": cotangent}


EXTINCTION = 0.7

def window_objective(window, cot_rows, light_dir, colour_tint):
    padded = jnp.pad(window, ((1, 1), (0, 0), (1, 1)))
    grad_x = (padded[2:, 1:-1, 1:-1] - padded[:-2, 1:-1, 1:-1]) * 0.5
    grad_y = (padded[1:-1, 2:, 1:-1] - padded[1:-1, :-2, 1:-1]) * 0.5
    grad_z = (padded[1:-1, 1:-1, 2:] - padded[1:-1, 1:-1, :-2]) * 0.5
    centre = window[:, 1:-1]
    radius = jnp.sqrt(1.0 + grad_x * grad_x + grad_y * grad_y + grad_z * grad_z)
    lit = light_dir[0] * grad_x + light_dir[1] * grad_y + light_dir[2] * grad_z
    shading = 0.5 + 0.5 * lit / radius
    optical = centre * (EXTINCTION / NDEP)
    transmit = jnp.exp(-(jnp.cumsum(optical, axis=0) - optical))
    weight = transmit * (1.0 - jnp.exp(-optical)) * centre * shading
    pixels = lax.optimization_barrier(jnp.sum(weight, axis=0))
    return jnp.sum(cot_rows * colour_tint[:, None, None] * pixels[None])

def reference(density, light_dir, colour_tint, cotangent):
    padded_rows = jnp.pad(density, ((0, 0), (2, 2), (0, 0)))
    padded_cot = jnp.pad(cotangent, ((0, 0), (1, 1), (0, 0)))
    gradient_fn = jax.grad(window_objective)

    def one_block(row_block):
        first_row = (row_block * 8).astype(jnp.int32)
        anchor = jnp.zeros((), jnp.int32)
        window = lax.dynamic_slice(padded_rows, (anchor, first_row, anchor), (NDEP, 12, NCOL))
        cot_rows = lax.dynamic_slice(padded_cot, (anchor, first_row, anchor), (3, 10, NCOL))
        return gradient_fn(window, cot_rows, light_dir, colour_tint)[:, 2:10]
    blocks = lax.map(one_block, jnp.arange(NROW // 8, dtype=jnp.int32))
    stacked = jnp.moveaxis(blocks, 0, 1).reshape(NDEP, NROW, NCOL)
    return stacked * float(NDEP)
```

```python
import functools

import jax
import jax.numpy as jnp
from jax import lax
from jax.experimental import pallas as pl
from jax.experimental.pallas import tpu as pltpu
from jax.sharding import PartitionSpec as P

EXTINCTION = 0.7
SUB = 8
LANE = 128
MESH = pl.DeviceIdType.MESH


def owners_of(tiles, n):
    own = min(n, tiles)
    while tiles % own:
        own -= 1
    return own


def kernel(
    n,
    m,
    light,
    tint,
    cot,
    dens_hbm,
    fa_hbm,
    e_out,
    D,
    W,
    U,
    INV,
    Q,
    DX,
    DY,
    DZ,
    CUM,
    AX,
    FA,
    PJ,
    FP,
    GS,
    xlo,
    xhi,
    axlo,
    axhi,
    rows_out,
    ylo,
    yhi,
    edge_out,
    aylo,
    ayhi,
    d_send,
    d_recv,
    d_res,
    d_back,
    v_send,
    v_recv,
    v_res,
    v_back,
    in_sem,
    out_sem,
    halo_ss,
    halo_rs,
    d_ss,
    d_rs,
    d_bs,
    d_br,
    v_ss,
    v_rs,
    v_bs,
    v_br,
):
    me = lax.axis_index("ray")
    mine = lax.axis_index("row")
    nd, rows, cols = dens_hbm.shape
    nr, nc = rows // SUB, cols // LANE
    full = nd * n
    step = EXTINCTION / full
    n_own = v_send.shape[0]
    tpo = nr * nc // n_own
    tiles = [(r, c) for c in range(nc) for r in range(nr)]
    chunks = in_sem.shape[0]
    per = nd // chunks

    def rs(r):
        return slice(r * SUB, (r + 1) * SUB)

    def cs(c):
        return slice(c * LANE, (c + 1) * LANE)

    barrier = pltpu.get_barrier_semaphore()
    for q in range(n):

        @pl.when(me != q)
        def _():
            pl.semaphore_signal(barrier, inc=1, device_id={"ray": q}, device_id_type=MESH)

    @pl.when(mine > 0)
    def _():
        pl.semaphore_signal(barrier, inc=1, device_id={"row": mine - 1}, device_id_type=MESH)

    @pl.when(mine < m - 1)
    def _():
        pl.semaphore_signal(barrier, inc=1, device_id={"row": mine + 1}, device_id_type=MESH)

    loads = [
        pltpu.make_async_copy(
            dens_hbm.at[pl.ds(i * per, per)], D.at[pl.ds(1 + i * per, per)], in_sem.at[i]
        )
        for i in range(chunks)
    ]
    for load in loads:
        load.start()
    for r, c in tiles:
        PJ[rs(r), cs(c)] = sum(cot[ch, rs(r), cs(c)] * tint[ch] for ch in range(3))
    for load in loads:
        load.wait()
    for k in range(nd):
        rows_out[0, k] = D[1 + k, 0:1, :]
        rows_out[1, k] = D[1 + k, rows - 1 : rows, :]

    def neighbours(layer_lo, layer_hi, x_lo, x_hi, edges, y_lo, y_hi, base):
        def copy(i, src, dst, where):
            return pltpu.make_async_remote_copy(
                src_ref=src,
                dst_ref=dst,
                send_sem=halo_ss.at[base + i],
                recv_sem=halo_rs.at[base + i],
                device_id=where,
                device_id_type=MESH,
            )

        return [
            (mine > 0, mine < m - 1, copy(0, edges.at[0], y_hi, {"row": jnp.maximum(mine - 1, 0)})),
            (mine < m - 1, mine > 0, copy(1, edges.at[1], y_lo, {"row": jnp.minimum(mine + 1, m - 1)})),
            (me > 0, me < n - 1, copy(2, layer_lo, x_hi, {"ray": jnp.maximum(me - 1, 0)})),
            (me < n - 1, me > 0, copy(3, layer_hi, x_lo, {"ray": jnp.minimum(me + 1, n - 1)})),
        ]

    def start_all(plan):
        for sends, _, copy in plan:
            pl.when(sends)(copy.start)

    def arrive(plan, empties):
        for (_, receives, copy), empty in zip(plan, empties):
            pl.when(receives)(copy.wait_recv)

            @pl.when(jnp.logical_not(receives))
            def _():
                empty[...] = jnp.zeros_like(empty)

    def sent(plan):
        for sends, _, copy in plan:
            pl.when(sends)(copy.wait_send)

    peers = (n - 1) + (mine > 0).astype(jnp.int32) + (mine < m - 1).astype(jnp.int32)
    pl.semaphore_wait(barrier, peers)

    dens_plan = neighbours(D.at[1], D.at[nd], xlo, xhi, rows_out, ylo, yhi, 0)
    start_all(dens_plan)

    def to_owner(o, send, recv, ss, rs_):
        return pltpu.make_async_remote_copy(
            src_ref=send.at[o],
            dst_ref=recv.at[me],
            send_sem=ss.at[o],
            recv_sem=rs_.at[me],
            device_id={"ray": o},
            device_id_type=MESH,
        )

    def from_peer(q, send, recv, ss, rs_):
        return pltpu.make_async_remote_copy(
            src_ref=send.at[0],
            dst_ref=recv.at[q],
            send_sem=ss.at[0],
            recv_sem=rs_.at[q],
            device_id={"ray": q},
            device_id_type=MESH,
        )

    def to_peer(q, res, back, bs, br):
        return pltpu.make_async_remote_copy(
            src_ref=res.at[q],
            dst_ref=back.at[me],
            send_sem=bs.at[q],
            recv_sem=br.at[me],
            device_id={"ray": q},
            device_id_type=MESH,
        )

    def from_owner(o, res, back, bs, br):
        return pltpu.make_async_remote_copy(
            src_ref=res.at[0],
            dst_ref=back.at[o],
            send_sem=bs.at[0],
            recv_sem=br.at[o],
            device_id={"ray": o},
            device_id_type=MESH,
        )

    def scatter(send, recv, ss, rs_):
        for o in range(n_own):

            @pl.when(me != o)
            def _():
                to_owner(o, send, recv, ss, rs_).start()

            @pl.when(me == o)
            def _():
                recv[o] = send[o]

    def combine(send, recv, res, back, ss, rs_, bs, br, total):
        mine_to_sum = me < n_own

        @pl.when(mine_to_sum)
        def _():
            for q in range(n):

                @pl.when(me != q)
                def _():
                    from_peer(q, send, recv, ss, rs_).wait_recv()

            total(recv, res)
            for q in range(n):

                @pl.when(me != q)
                def _():
                    to_peer(q, res, back, bs, br).start()

                if q < n_own:

                    @pl.when(me == q)
                    def _():
                        back[q] = res[q]

    def collect(res, back, bs, br):
        for o in range(n_own):

            @pl.when(me != o)
            def _():
                from_owner(o, res, back, bs, br).wait_recv()

    def finish(send, recv, res, back, ss, rs_, bs, br):
        for o in range(n_own):

            @pl.when(me != o)
            def _():
                to_owner(o, send, recv, ss, rs_).wait_send()

        @pl.when(me < n_own)
        def _():
            for q in range(n):

                @pl.when(me != q)
                def _():
                    to_peer(q, res, back, bs, br).wait_send()

    def slot(i):
        return i // tpo, slice((i % tpo) * SUB, (i % tpo + 1) * SUB)

    def pass_a(k, carry):
        trans, depth = carry
        new_trans, new_depth = [], []
        for i, (r, c) in enumerate(tiles):
            d = D[k + 1, rs(r), cs(c)]
            o = d * step
            p = jnp.exp(-o)
            op = 1.0 - p
            W[k, rs(r), cs(c)] = trans[i] * (op * d)
            U[k, rs(r), cs(c)] = trans[i] * ((op + o * p) * float(full))
            new_trans.append(trans[i] * p)
            new_depth.append(depth[i] + o)
        return new_trans, new_depth

    ones = [jnp.ones((SUB, LANE), jnp.float32) for _ in tiles]
    zeros = [jnp.zeros((SUB, LANE), jnp.float32) for _ in tiles]
    _, depth = lax.fori_loop(0, nd, pass_a, (ones, zeros))
    for i, _ in enumerate(tiles):
        o, s = slot(i)
        d_send[o, s, :] = depth[i]
    scatter(d_send, d_recv, d_ss, d_rs)

    arrive(dens_plan, (yhi, ylo, xhi, xlo))
    for r, c in tiles:
        D[0, rs(r), cs(c)] = xlo[rs(r), cs(c)]
        D[nd + 1, rs(r), cs(c)] = xhi[rs(r), cs(c)]

    lane = lax.broadcasted_iota(jnp.int32, (SUB, LANE), 1)
    sub = lax.broadcasted_iota(jnp.int32, (SUB, LANE), 0)
    first_lane, last_lane = lane == 0, lane == LANE - 1
    first_sub, last_sub = sub == 0, sub == SUB - 1

    def along_cols(row_of_tiles):
        ahead = [pltpu.roll(t, 1, 1) for t in row_of_tiles]
        after = [pltpu.roll(t, LANE - 1, 1) for t in row_of_tiles]
        prev = [jnp.where(first_lane, ahead[c - 1] if c else 0.0, ahead[c]) for c in range(nc)]
        nxt = [
            jnp.where(last_lane, after[c + 1] if c < nc - 1 else 0.0, after[c]) for c in range(nc)
        ]
        return prev, nxt

    def along_rows(col_of_tiles, above, below):
        down = [pltpu.roll(t, 1, 0) for t in col_of_tiles]
        up = [pltpu.roll(t, SUB - 1, 0) for t in col_of_tiles]
        prev = [jnp.where(first_sub, down[r - 1] if r else above, down[r]) for r in range(nr)]
        nxt = [jnp.where(last_sub, up[r + 1] if r < nr - 1 else below, up[r]) for r in range(nr)]
        return prev, nxt

    def wide(ref, k, c):
        return jnp.broadcast_to(ref[k, :, cs(c)], (SUB, LANE))

    half = [light[a] * 0.5 for a in range(3)]

    def pass_b(k, total):
        here = {(r, c): D[k + 1, rs(r), cs(c)] for r, c in tiles}
        z = [along_cols([here[r, c] for c in range(nc)]) for r in range(nr)]
        new = []
        for c in range(nc):
            prev, nxt = along_rows(
                [here[r, c] for r in range(nr)], wide(ylo, k, c), wide(yhi, k, c)
            )
            for r in range(nr):
                at = (k, rs(r), cs(c))
                dx = D[k + 2, rs(r), cs(c)] - D[k, rs(r), cs(c)]
                dy = nxt[r] - prev[r]
                dz = z[r][1][c] - z[r][0][c]
                inv = lax.rsqrt(1.0 + 0.25 * (dx * dx + dy * dy + dz * dz))
                q = (half[0] * dx + half[1] * dy + half[2] * dz) * inv
                now = total[len(new)] + W[at] * (0.5 + 0.5 * q)
                DX[at] = dx
                DY[at] = dy
                DZ[at] = dz
                INV[at] = inv
                Q[at] = q
                CUM[at] = now
                new.append(now)
        return new

    cut = nd // 2
    emitted = lax.fori_loop(0, cut, pass_b, zeros)

    def before(recv, res):
        acc = jnp.zeros(recv.shape[1:], jnp.float32)
        for q in range(n):
            res[q] = acc
            acc = acc + recv[q]

    combine(d_send, d_recv, d_res, d_back, d_ss, d_rs, d_bs, d_br, before)
    emitted = lax.fori_loop(cut, nd, pass_b, emitted)
    collect(d_res, d_back, d_bs, d_br)
    for i, (r, c) in enumerate(tiles):
        o, s = slot(i)
        fp = jnp.exp(-d_back[o, s, :]) * PJ[rs(r), cs(c)]
        FP[rs(r), cs(c)] = fp
        GS[rs(r), cs(c)] = fp * (0.25 * full)
        v_send[o, s, :] = fp * emitted[i]
    scatter(v_send, v_recv, v_ss, v_rs)

    def pass_c(k, carry):
        for c in range(nc):
            for r in range(nr):
                at = (k, rs(r), cs(c))
                inv = INV[at]
                s = GS[rs(r), cs(c)] * W[at] * inv
                b = s * (Q[at] * inv) * 0.5
                AX[k + 1, rs(r), cs(c)] = s * light[0] - b * DX[at]
                ay = s * light[1] - b * DY[at]
                DY[at] = ay
                DZ[at] = s * light[2] - b * DZ[at]
                if r == 0:
                    edge_out[0, k, :, cs(c)] = ay[0:1]
                if r == nr - 1:
                    edge_out[1, k, :, cs(c)] = ay[SUB - 1 : SUB]
        return carry

    lax.fori_loop(0, nd, pass_c, 0)
    adj_plan = neighbours(AX.at[1], AX.at[nd], axlo, axhi, edge_out, aylo, ayhi, 4)
    start_all(adj_plan)

    def beyond(recv, res):
        acc = jnp.zeros(recv.shape[1:], jnp.float32)
        for q in reversed(range(n)):
            acc = acc + recv[q]
            res[q] = acc * EXTINCTION

    combine(v_send, v_recv, v_res, v_back, v_ss, v_rs, v_bs, v_br, beyond)
    arrive(adj_plan, (ayhi, aylo, axhi, axlo))
    for r, c in tiles:
        AX[0, rs(r), cs(c)] = axlo[rs(r), cs(c)]
        AX[nd + 1, rs(r), cs(c)] = axhi[rs(r), cs(c)]

    def pass_d(k, carry):
        z = [along_cols([DZ[k, rs(r), cs(c)] for c in range(nc)]) for r in range(nr)]
        for c in range(nc):
            prev, nxt = along_rows(
                [DY[k, rs(r), cs(c)] for r in range(nr)], wide(aylo, k, c), wide(ayhi, k, c)
            )
            for r in range(nr):
                at = (k, rs(r), cs(c))
                own = FP[rs(r), cs(c)] * (U[at] * (0.5 + 0.5 * Q[at]) + EXTINCTION * CUM[at])
                fx = AX[k, rs(r), cs(c)] - AX[k + 2, rs(r), cs(c)]
                FA[at] = own + fx + (prev[r] - nxt[r]) + (z[r][0][c] - z[r][1][c])
        return carry

    stores = []
    for i in range(chunks):
        lax.fori_loop(i * per, (i + 1) * per, pass_d, 0)
        part = pl.ds(i * per, per)
        stores.append(pltpu.make_async_copy(FA.at[part], fa_hbm.at[part], out_sem.at[i]))
        stores[-1].start()

    collect(v_res, v_back, v_bs, v_br)
    for i, (r, c) in enumerate(tiles):
        o, s = slot(i)
        e_out[rs(r), cs(c)] = v_back[o, s, :]
    for store in stores:
        store.wait()
    sent(dens_plan)
    sent(adj_plan)
    finish(d_send, d_recv, d_res, d_back, d_ss, d_rs, d_bs, d_br)
    finish(v_send, v_recv, v_res, v_back, v_ss, v_rs, v_bs, v_br)


def local(n, m, density, light_dir, colour_tint, cotangent):
    nd, rows, cols = density.shape
    tiles = (rows // SUB) * (cols // LANE)
    n_own = owners_of(tiles, n)
    chunk = (tiles // n_own * SUB, LANE)
    chunks = 4 if nd % 4 == 0 else 1
    f32 = jnp.float32

    def vmem(*shape):
        return pltpu.VMEM(shape, f32)

    dma = pltpu.SemaphoreType.DMA
    volume = vmem(nd, rows, cols)
    padded = vmem(nd + 2, rows, cols)
    layer = vmem(rows, cols)
    side = vmem(nd, 1, cols)
    scan = [
        vmem(n_own, *chunk),
        vmem(n, *chunk),
        vmem(n, *chunk),
        vmem(n_own, *chunk),
    ]
    scan_sems = [dma((n_own,)), dma((n,)), dma((n,)), dma((n_own,))]
    scratch = (
        [padded]
        + [volume] * 8
        + [padded, volume]
        + [layer] * 3
        + [layer] * 4
        + [vmem(2, nd, 1, cols), side, side]
        + [vmem(2, nd, 1, cols), side, side]
        + scan
        + scan
        + [dma((chunks,)), dma((chunks,)), dma((8,)), dma((8,))]
        + scan_sems
        + scan_sems
    )
    fa, e = pl.pallas_call(
        functools.partial(kernel, n, m),
        out_shape=(
            jax.ShapeDtypeStruct((nd, rows, cols), f32),
            jax.ShapeDtypeStruct((rows, cols), f32),
        ),
        in_specs=[
            pl.BlockSpec(memory_space=pltpu.SMEM),
            pl.BlockSpec(memory_space=pltpu.SMEM),
            pl.BlockSpec(memory_space=pltpu.VMEM),
            pl.BlockSpec(memory_space=pl.ANY),
        ],
        out_specs=(pl.BlockSpec(memory_space=pl.ANY), pl.BlockSpec(memory_space=pltpu.VMEM)),
        scratch_shapes=scratch,
        compiler_params=pltpu.CompilerParams(
            collective_id=0, has_side_effects=True, vmem_limit_bytes=48 * 2**20
        ),
        name="render_grad",
    )(light_dir, colour_tint, cotangent, density)
    return fa - e[None]


def solution(mesh):
    placed = (P("ray", "row", None), P(), P(), P(None, "row", None))
    return jax.shard_map(
        functools.partial(local, mesh.shape["ray"], mesh.shape["row"]),
        mesh=mesh,
        in_specs=placed,
        out_specs=P("ray", "row", None),
        check_vma=False,
    )
```

```python
import functools

import jax
import jax.numpy as jnp
from jax import lax
from jax.experimental import pallas as pl
from jax.experimental.pallas import tpu as pltpu
from jax.sharding import PartitionSpec as P

EXTINCTION = 0.7
SUB = 8
LANE = 128
MESH = pl.DeviceIdType.MESH


def owners_of(tiles, n):
    own = min(n, tiles)
    while tiles % own:
        own -= 1
    return own


def kernel(
    n,
    m,
    off,
    light_hbm,
    tint_hbm,
    cot_hbm,
    dens_hbm,
    fa_hbm,
    e_out,
    light,
    tint,
    cot,
    D,
    W,
    U,
    INV,
    Q,
    DX,
    DY,
    DZ,
    CUM,
    AX,
    FA,
    PJ,
    FR,
    E0,
    xlo,
    xhi,
    axlo,
    axhi,
    axsend,
    rows_out,
    ylo,
    yhi,
    edge_out,
    aylo,
    ayhi,
    front_out,
    flo,
    fhi,
    d_send,
    d_recv,
    d_res,
    d_back,
    v_send,
    v_recv,
    v_res,
    v_back,
    in_sem,
    out_sem,
    small_sem,
    halo_ss,
    halo_rs,
    d_ss,
    d_rs,
    d_bs,
    d_br,
    v_ss,
    v_rs,
    v_bs,
    v_br,
):
    me = lax.axis_index("ray")
    mine = lax.axis_index("row")
    nd, rows, cols = dens_hbm.shape
    nr, nc = rows // SUB, cols // LANE
    full = nd * n
    step = EXTINCTION / full
    n_own = v_send.shape[0]
    tpo = nr * nc // n_own
    tiles = [(r, c) for c in range(nc) for r in range(nr)]
    chunks = in_sem.shape[0]
    per = nd // chunks

    def rs(r):
        return slice(r * SUB, (r + 1) * SUB)

    def cs(c):
        return slice(c * LANE, (c + 1) * LANE)

    barrier = pltpu.get_barrier_semaphore()
    for q in range(n):

        @pl.when(me != q)
        def _():
            pl.semaphore_signal(barrier, inc=1, device_id={"ray": q}, device_id_type=MESH)

    @pl.when(mine > 0)
    def _():
        pl.semaphore_signal(barrier, inc=1, device_id={"row": mine - 1}, device_id_type=MESH)

    @pl.when(mine < m - 1)
    def _():
        pl.semaphore_signal(barrier, inc=1, device_id={"row": mine + 1}, device_id_type=MESH)

    loads = [
        pltpu.make_async_copy(
            dens_hbm.at[pl.ds(i * per, per)], D.at[pl.ds(1 + i * per, per)], in_sem.at[i]
        )
        for i in range(chunks)
    ]
    small = [
        pltpu.make_async_copy(light_hbm, light, small_sem.at[0]),
        pltpu.make_async_copy(tint_hbm, tint, small_sem.at[1]),
        pltpu.make_async_copy(cot_hbm, cot, small_sem.at[2]),
    ]
    for load in loads + small:
        load.start()
    for i, load in enumerate(loads):
        load.wait()
        for k in range(i * per, (i + 1) * per):
            rows_out[0, k] = D[1 + k, 0:1, :]
            rows_out[1, k] = D[1 + k, rows - 1 : rows, :]

    used = [0]

    def link(to, src, dst):
        axis, by = to
        here, last = (mine, m - 1) if axis == "row" else (me, n - 1)
        if by < 0:
            sends, receives, where = here > 0, here < last, jnp.maximum(here - 1, 0)
        else:
            sends, receives, where = here < last, here > 0, jnp.minimum(here + 1, last)
        i = used[0]
        used[0] += 1
        copy = pltpu.make_async_remote_copy(
            src_ref=src,
            dst_ref=dst,
            send_sem=halo_ss.at[i],
            recv_sem=halo_rs.at[i],
            device_id={axis: where},
            device_id_type=MESH,
        )
        return sends, receives, copy, dst

    up, down, near, far = ("row", -1), ("row", 1), ("ray", -1), ("ray", 1)
    every = []

    def start_all(plan):
        every.extend(plan)
        for sends, _, copy, _ in plan:
            pl.when(sends)(copy.start)

    def arrive(plan):
        for _, receives, copy, dst in plan:
            pl.when(receives)(copy.wait_recv)

            @pl.when(jnp.logical_not(receives))
            def _():
                dst[...] = jnp.zeros(dst.shape, jnp.float32)

    def to_owner(o, send, recv, ss, rs_):
        return pltpu.make_async_remote_copy(
            src_ref=send.at[o],
            dst_ref=recv.at[me],
            send_sem=ss.at[o],
            recv_sem=rs_.at[me],
            device_id={"ray": off + o},
            device_id_type=MESH,
        )

    def from_peer(q, send, recv, ss, rs_):
        return pltpu.make_async_remote_copy(
            src_ref=send.at[0],
            dst_ref=recv.at[q],
            send_sem=ss.at[0],
            recv_sem=rs_.at[q],
            device_id={"ray": q},
            device_id_type=MESH,
        )

    def to_peer(q, res, back, bs, br):
        mine_as_owner = jnp.clip(me - off, 0, n_own - 1)
        return pltpu.make_async_remote_copy(
            src_ref=res.at[q],
            dst_ref=back.at[mine_as_owner],
            send_sem=bs.at[q],
            recv_sem=br.at[mine_as_owner],
            device_id={"ray": q},
            device_id_type=MESH,
        )

    def from_owner(o, res, back, bs, br):
        return pltpu.make_async_remote_copy(
            src_ref=res.at[0],
            dst_ref=back.at[o],
            send_sem=bs.at[0],
            recv_sem=br.at[o],
            device_id={"ray": off + o},
            device_id_type=MESH,
        )

    owner = jnp.logical_and(me >= off, me < off + n_own)

    def scatter(send, recv, ss, rs_):
        for o in range(n_own):

            @pl.when(me != off + o)
            def _():
                to_owner(o, send, recv, ss, rs_).start()

            @pl.when(me == off + o)
            def _():
                recv[off + o] = send[o]

    def combine(send, recv, res, back, ss, rs_, bs, br, total):
        @pl.when(owner)
        def _():
            for q in range(n):

                @pl.when(me != q)
                def _():
                    from_peer(q, send, recv, ss, rs_).wait_recv()

            total()
            for q in range(n):

                @pl.when(me != q)
                def _():
                    to_peer(q, res, back, bs, br).start()

                if off <= q < off + n_own:

                    @pl.when(me == q)
                    def _():
                        back[q - off] = res[q]

    def collect(res, back, bs, br):
        for o in range(n_own):

            @pl.when(me != off + o)
            def _():
                from_owner(o, res, back, bs, br).wait_recv()

    def finish(send, recv, res, back, ss, rs_, bs, br):
        for o in range(n_own):

            @pl.when(me != off + o)
            def _():
                to_owner(o, send, recv, ss, rs_).wait_send()

        @pl.when(owner)
        def _():
            for q in range(n):

                @pl.when(me != q)
                def _():
                    to_peer(q, res, back, bs, br).wait_send()

    def slot(i):
        return i // tpo, slice((i % tpo) * SUB, (i % tpo + 1) * SUB)

    def pass_a(k, carry):
        trans, depth = carry
        new_trans, new_depth = [], []
        for i, (r, c) in enumerate(tiles):
            d = D[k + 1, rs(r), cs(c)]
            o = d * step
            p = jnp.exp(-o)
            op = 1.0 - p
            W[k, rs(r), cs(c)] = trans[i] * (op * d)
            U[k, rs(r), cs(c)] = trans[i] * ((op + o * p) * float(full))
            new_trans.append(trans[i] * p)
            new_depth.append(depth[i] + o)
        return new_trans, new_depth

    ones = [jnp.ones((SUB, LANE), jnp.float32) for _ in tiles]
    zeros = [jnp.zeros((SUB, LANE), jnp.float32) for _ in tiles]
    _, depth = lax.fori_loop(0, nd, pass_a, (ones, zeros))
    for i, _ in enumerate(tiles):
        o, s = slot(i)
        d_send[o, s, :] = depth[i]

    peers = (n - 1) + (mine > 0).astype(jnp.int32) + (mine < m - 1).astype(jnp.int32)
    pl.semaphore_wait(barrier, peers)

    side_plans = []
    for i in range(chunks):
        part = pl.ds(i * per, per)
        side_plans.append(
            [
                link(up, rows_out.at[0, part], yhi.at[part]),
                link(down, rows_out.at[1, part], ylo.at[part]),
            ]
        )
        start_all(side_plans[-1])
    layer_plan = [link(near, D.at[1], xhi), link(far, D.at[nd], xlo)]
    start_all(layer_plan)
    scatter(d_send, d_recv, d_ss, d_rs)

    for load in small:
        load.wait()
    for r, c in tiles:
        PJ[rs(r), cs(c)] = sum(cot[ch, rs(r), cs(c)] * tint[ch] for ch in range(3))

    lane = lax.broadcasted_iota(jnp.int32, (SUB, LANE), 1)
    sub = lax.broadcasted_iota(jnp.int32, (SUB, LANE), 0)
    first_lane, last_lane = lane == 0, lane == LANE - 1
    first_sub, last_sub = sub == 0, sub == SUB - 1

    def along_cols(row_of_tiles):
        ahead = [pltpu.roll(t, 1, 1) for t in row_of_tiles]
        after = [pltpu.roll(t, LANE - 1, 1) for t in row_of_tiles]
        prev = [jnp.where(first_lane, ahead[c - 1] if c else 0.0, ahead[c]) for c in range(nc)]
        nxt = [
            jnp.where(last_lane, after[c + 1] if c < nc - 1 else 0.0, after[c]) for c in range(nc)
        ]
        return prev, nxt

    def along_rows(col_of_tiles, above, below):
        down_ = [pltpu.roll(t, 1, 0) for t in col_of_tiles]
        up_ = [pltpu.roll(t, SUB - 1, 0) for t in col_of_tiles]
        prev = [jnp.where(first_sub, down_[r - 1] if r else above, down_[r]) for r in range(nr)]
        nxt = [jnp.where(last_sub, up_[r + 1] if r < nr - 1 else below, up_[r]) for r in range(nr)]
        return prev, nxt

    def wide(row):
        return jnp.broadcast_to(row, (SUB, LANE))

    half = [light[a] * 0.5 for a in range(3)]

    def pass_b(k, total, at_first=False):
        here = {(r, c): D[k + 1, rs(r), cs(c)] for r, c in tiles}
        z = [along_cols([here[r, c] for c in range(nc)]) for r in range(nr)]
        new = []
        for c in range(nc):
            prev, nxt = along_rows(
                [here[r, c] for r in range(nr)], wide(ylo[k, :, cs(c)]), wide(yhi[k, :, cs(c)])
            )
            for r in range(nr):
                at = (k, rs(r), cs(c))
                ahead = xlo[rs(r), cs(c)] if at_first else D[k, rs(r), cs(c)]
                dx = D[k + 2, rs(r), cs(c)] - ahead
                dy = nxt[r] - prev[r]
                dz = z[r][1][c] - z[r][0][c]
                inv = lax.rsqrt(1.0 + 0.25 * (dx * dx + dy * dy + dz * dz))
                q = (half[0] * dx + half[1] * dy + half[2] * dz) * inv
                here_now = W[at] * (0.5 + 0.5 * q)
                now = total[len(new)] + here_now
                DX[at] = dx
                DY[at] = dy
                DZ[at] = dz
                INV[at] = inv
                Q[at] = q
                if at_first:
                    E0[rs(r), cs(c)] = here_now
                    CUM[at] = jnp.zeros((SUB, LANE), jnp.float32)
                else:
                    CUM[at] = now
                new.append(now)
        return new

    emitted = zeros
    for i in range(chunks):
        arrive(side_plans[i])
        lo = max(i * per, 1)
        hi = min((i + 1) * per, nd - 1)
        emitted = lax.fori_loop(lo, hi, pass_b, emitted)
    arrive(layer_plan)
    for r, c in tiles:
        D[nd + 1, rs(r), cs(c)] = xhi[rs(r), cs(c)]
    emitted = pass_b(nd - 1, emitted)
    emitted = pass_b(0, emitted, True)
    for i, (r, c) in enumerate(tiles):
        o, s = slot(i)
        v_send[o, s, :] = PJ[rs(r), cs(c)] * emitted[i]
    scatter(v_send, v_recv, v_ss, v_rs)

    def fronts():
        acc = jnp.zeros(d_recv.shape[1:], jnp.float32)
        for q in range(n):
            d_res[q] = jnp.exp(-acc)
            acc = acc + d_recv[q]

    combine(d_send, d_recv, d_res, d_back, d_ss, d_rs, d_bs, d_br, fronts)

    def pass_c(k, carry):
        for c in range(nc):
            for r in range(nr):
                at = (k, rs(r), cs(c))
                inv = INV[at]
                s = (PJ[rs(r), cs(c)] * (0.25 * full)) * W[at] * inv
                b = s * (Q[at] * inv) * 0.5
                AX[k + 1, rs(r), cs(c)] = s * light[0] - b * DX[at]
                ay = s * light[1] - b * DY[at]
                DY[at] = ay
                DZ[at] = s * light[2] - b * DZ[at]
                if r == 0:
                    edge_out[0, k, :, cs(c)] = ay[0:1]
                if r == nr - 1:
                    edge_out[1, k, :, cs(c)] = ay[SUB - 1 : SUB]
        return carry

    lax.fori_loop(0, nd, pass_c, 0)
    for i, (r, c) in enumerate(tiles):
        o, s = slot(i)
        axsend[rs(r), cs(c)] = AX[nd, rs(r), cs(c)] * jnp.exp(d_send[o, s, :])
    adj_plan = [
        link(up, edge_out.at[0], ayhi),
        link(down, edge_out.at[1], aylo),
        link(near, AX.at[1], axhi),
        link(far, axsend, axlo),
    ]
    start_all(adj_plan)

    def beyond():
        acc = jnp.zeros(v_recv.shape[1:], jnp.float32)
        for q in reversed(range(n)):
            acc = acc + d_res[q] * v_recv[q]
            v_res[q] = acc * EXTINCTION

    def value_combine():
        combine(v_send, v_recv, v_res, v_back, v_ss, v_rs, v_bs, v_br, beyond)

    collect(d_res, d_back, d_bs, d_br)
    for i, (r, c) in enumerate(tiles):
        o, s = slot(i)
        FR[rs(r), cs(c)] = d_back[o, s, :]
    front_out[0] = FR[0:1, :]
    front_out[1] = FR[rows - 1 : rows, :]
    front_plan = [link(up, front_out.at[0], fhi), link(down, front_out.at[1], flo)]
    start_all(front_plan)
    value_combine()

    def pass_d(k, carry):
        fr = {(r, c): FR[rs(r), cs(c)] for r, c in tiles}
        z = [
            along_cols([fr[r, c] * DZ[k, rs(r), cs(c)] for c in range(nc)]) for r in range(nr)
        ]
        for c in range(nc):
            prev, nxt = along_rows(
                [fr[r, c] * DY[k, rs(r), cs(c)] for r in range(nr)], 0.0, 0.0
            )
            for r in range(nr):
                at = (k, rs(r), cs(c))
                own = PJ[rs(r), cs(c)] * (U[at] * (0.5 + 0.5 * Q[at]) + EXTINCTION * CUM[at])
                fx = AX[k, rs(r), cs(c)] - AX[k + 2, rs(r), cs(c)]
                FA[at] = fr[r, c] * (own + fx) + (prev[r] - nxt[r]) + (z[r][0][c] - z[r][1][c])
        return carry

    lax.fori_loop(1, nd - 1, pass_d, 0)
    arrive(adj_plan)
    for i, (r, c) in enumerate(tiles):
        o, s = slot(i)
        AX[0, rs(r), cs(c)] = axlo[rs(r), cs(c)]
        AX[nd + 1, rs(r), cs(c)] = axhi[rs(r), cs(c)] * jnp.exp(-d_send[o, s, :])
    lax.fori_loop(0, 2, lambda i, carry: pass_d(i * (nd - 1), carry), 0)
    arrive(front_plan)

    def pass_e(k, carry):
        for c in range(nc):
            top = wide(flo[:, cs(c)] * aylo[k, :, cs(c)])
            at = (k, rs(0), cs(c))
            FA[at] = FA[at] + jnp.where(first_sub, top, 0.0)
            bottom = wide(fhi[:, cs(c)] * ayhi[k, :, cs(c)])
            at = (k, rs(nr - 1), cs(c))
            FA[at] = FA[at] - jnp.where(last_sub, bottom, 0.0)
        return carry

    stores = []
    for i in range(chunks):
        lax.fori_loop(i * per, (i + 1) * per, pass_e, 0)
        part = pl.ds(i * per, per)
        stores.append(pltpu.make_async_copy(FA.at[part], fa_hbm.at[part], out_sem.at[i]))
        stores[-1].start()

    collect(v_res, v_back, v_bs, v_br)
    for i, (r, c) in enumerate(tiles):
        o, s = slot(i)
        at = (rs(r), cs(c))
        e_out[at] = v_back[o, s, :] - EXTINCTION * (FR[at] * (PJ[at] * E0[at]))
    for store in stores:
        store.wait()
    for sends, _, copy, _ in every:
        pl.when(sends)(copy.wait_send)
    finish(d_send, d_recv, d_res, d_back, d_ss, d_rs, d_bs, d_br)
    finish(v_send, v_recv, v_res, v_back, v_ss, v_rs, v_bs, v_br)


def local(n, m, density, light_dir, colour_tint, cotangent):
    nd, rows, cols = density.shape
    tiles = (rows // SUB) * (cols // LANE)
    n_own = owners_of(tiles, max(n // 2, 1))
    off = (n - n_own) // 2
    chunk = (tiles // n_own * SUB, LANE)
    chunks = 4 if nd % 4 == 0 else 1
    f32 = jnp.float32

    def vmem(*shape):
        return pltpu.VMEM(shape, f32)

    dma = pltpu.SemaphoreType.DMA
    volume = vmem(nd, rows, cols)
    padded = vmem(nd + 2, rows, cols)
    layer = vmem(rows, cols)
    side = vmem(nd, 1, cols)
    scan = [
        vmem(n_own, *chunk),
        vmem(n, *chunk),
        vmem(n, *chunk),
        vmem(n_own, *chunk),
    ]
    scan_sems = [dma((n_own,)), dma((n,)), dma((n,)), dma((n_own,))]
    links = 2 * chunks + 8
    scratch = (
        [pltpu.SMEM(light_dir.shape, f32), pltpu.SMEM(colour_tint.shape, f32)]
        + [vmem(*cotangent.shape), padded]
        + [volume] * 8
        + [padded, volume]
        + [layer] * 3
        + [layer] * 5
        + [vmem(2, nd, 1, cols), side, side]
        + [vmem(2, nd, 1, cols), side, side]
        + [vmem(2, 1, cols), vmem(1, cols), vmem(1, cols)]
        + scan
        + scan
        + [dma((chunks,)), dma((chunks,)), dma((3,)), dma((links,)), dma((links,))]
        + scan_sems
        + scan_sems
    )
    hbm = pl.BlockSpec(memory_space=pltpu.HBM)
    fa, e = pl.pallas_call(
        functools.partial(kernel, n, m, off),
        out_shape=(
            jax.ShapeDtypeStruct((nd, rows, cols), f32),
            jax.ShapeDtypeStruct((rows, cols), f32),
        ),
        in_specs=[hbm, hbm, hbm, hbm],
        out_specs=(
            hbm,
            pl.BlockSpec(memory_space=pltpu.VMEM),
        ),
        scratch_shapes=scratch,
        compiler_params=pltpu.CompilerParams(
            collective_id=0, has_side_effects=True, vmem_limit_bytes=64_000_000
        ),
        name="render_grad",
    )(light_dir, colour_tint, cotangent, density)
    return fa - e[None]


def solution(mesh):
    placed = (P("ray", "row", None), P(), P(), P(None, "row", None))
    return jax.shard_map(
        functools.partial(local, mesh.shape["ray"], mesh.shape["row"]),
        mesh=mesh,
        in_specs=placed,
        out_specs=P("ray", "row", None),
        check_vma=False,
    )
```

```python
import functools

import jax
import jax.numpy as jnp
from jax import lax
from jax.experimental import pallas as pl
from jax.experimental.pallas import tpu as pltpu
from jax.sharding import PartitionSpec as P

EXTINCTION = 0.7
SUB = 8
LANE = 128
MESH = pl.DeviceIdType.MESH


def owners_of(tiles, n):
    own = min(n, tiles)
    while tiles % own:
        own -= 1
    return own


def kernel(
    n,
    m,
    off,
    light_hbm,
    tint_hbm,
    cot_hbm,
    dens_hbm,
    FA,
    e_out,
    light,
    tint,
    cot,
    D,
    W,
    U,
    INV,
    Q,
    DX,
    DY,
    DZ,
    CUM,
    AX,
    PJ,
    FR,
    E0,
    xlo,
    xhi,
    axlo,
    axhi,
    axsend,
    rows_out,
    ylo,
    yhi,
    edge_out,
    aylo,
    ayhi,
    front_out,
    flo,
    fhi,
    d_send,
    d_recv,
    d_res,
    d_back,
    v_send,
    v_recv,
    v_res,
    v_back,
    in_sem,
    small_sem,
    halo_ss,
    halo_rs,
    d_ss,
    d_rs,
    d_bs,
    d_br,
    v_ss,
    v_rs,
    v_bs,
    v_br,
):
    me = lax.axis_index("ray")
    mine = lax.axis_index("row")
    nd, rows, cols = dens_hbm.shape
    nr, nc = rows // SUB, cols // LANE
    full = nd * n
    step = EXTINCTION / full
    n_own = v_send.shape[0]
    tpo = nr * nc // n_own
    tiles = [(r, c) for c in range(nc) for r in range(nr)]
    chunks = in_sem.shape[0]
    per = nd // chunks

    def rs(r):
        return slice(r * SUB, (r + 1) * SUB)

    def cs(c):
        return slice(c * LANE, (c + 1) * LANE)

    barrier = pltpu.get_barrier_semaphore()
    for q in range(n):

        @pl.when(me != q)
        def _():
            pl.semaphore_signal(barrier, inc=1, device_id={"ray": q}, device_id_type=MESH)

    @pl.when(mine > 0)
    def _():
        pl.semaphore_signal(barrier, inc=1, device_id={"row": mine - 1}, device_id_type=MESH)

    @pl.when(mine < m - 1)
    def _():
        pl.semaphore_signal(barrier, inc=1, device_id={"row": mine + 1}, device_id_type=MESH)

    loads = [
        pltpu.make_async_copy(
            dens_hbm.at[pl.ds(i * per, per)], D.at[pl.ds(1 + i * per, per)], in_sem.at[i]
        )
        for i in range(chunks)
    ]
    small = [
        pltpu.make_async_copy(light_hbm, light, small_sem.at[0]),
        pltpu.make_async_copy(tint_hbm, tint, small_sem.at[1]),
        pltpu.make_async_copy(cot_hbm, cot, small_sem.at[2]),
    ]
    for load in loads + small:
        load.start()
    for i, load in enumerate(loads):
        load.wait()
        for k in range(i * per, (i + 1) * per):
            rows_out[0, k] = D[1 + k, 0:1, :]
            rows_out[1, k] = D[1 + k, rows - 1 : rows, :]

    used = [0]

    def link(to, src, dst):
        axis, by = to
        here, last = (mine, m - 1) if axis == "row" else (me, n - 1)
        if by < 0:
            sends, receives, where = here > 0, here < last, jnp.maximum(here - 1, 0)
        else:
            sends, receives, where = here < last, here > 0, jnp.minimum(here + 1, last)
        i = used[0]
        used[0] += 1
        copy = pltpu.make_async_remote_copy(
            src_ref=src,
            dst_ref=dst,
            send_sem=halo_ss.at[i],
            recv_sem=halo_rs.at[i],
            device_id={axis: where},
            device_id_type=MESH,
        )
        return sends, receives, copy, dst

    up, down, near, far = ("row", -1), ("row", 1), ("ray", -1), ("ray", 1)
    every = []

    def start_all(plan):
        every.extend(plan)
        for sends, _, copy, _ in plan:
            pl.when(sends)(copy.start)

    def arrive(plan):
        for _, receives, copy, dst in plan:
            pl.when(receives)(copy.wait_recv)

            @pl.when(jnp.logical_not(receives))
            def _():
                dst[...] = jnp.zeros(dst.shape, jnp.float32)

    def to_owner(o, send, recv, ss, rs_):
        return pltpu.make_async_remote_copy(
            src_ref=send.at[o],
            dst_ref=recv.at[me],
            send_sem=ss.at[o],
            recv_sem=rs_.at[me],
            device_id={"ray": off + o},
            device_id_type=MESH,
        )

    def from_peer(q, send, recv, ss, rs_):
        return pltpu.make_async_remote_copy(
            src_ref=send.at[0],
            dst_ref=recv.at[q],
            send_sem=ss.at[0],
            recv_sem=rs_.at[q],
            device_id={"ray": q},
            device_id_type=MESH,
        )

    def to_peer(q, res, back, bs, br):
        mine_as_owner = jnp.clip(me - off, 0, n_own - 1)
        return pltpu.make_async_remote_copy(
            src_ref=res.at[q],
            dst_ref=back.at[mine_as_owner],
            send_sem=bs.at[q],
            recv_sem=br.at[mine_as_owner],
            device_id={"ray": q},
            device_id_type=MESH,
        )

    def from_owner(o, res, back, bs, br):
        return pltpu.make_async_remote_copy(
            src_ref=res.at[0],
            dst_ref=back.at[o],
            send_sem=bs.at[0],
            recv_sem=br.at[o],
            device_id={"ray": off + o},
            device_id_type=MESH,
        )

    owner = jnp.logical_and(me >= off, me < off + n_own)

    def scatter(send, recv, ss, rs_):
        for o in range(n_own):

            @pl.when(me != off + o)
            def _():
                to_owner(o, send, recv, ss, rs_).start()

            @pl.when(me == off + o)
            def _():
                recv[off + o] = send[o]

    def combine(send, recv, res, back, ss, rs_, bs, br, total):
        @pl.when(owner)
        def _():
            for q in range(n):

                @pl.when(me != q)
                def _():
                    from_peer(q, send, recv, ss, rs_).wait_recv()

            total()
            for q in range(n):

                @pl.when(me != q)
                def _():
                    to_peer(q, res, back, bs, br).start()

                if off <= q < off + n_own:

                    @pl.when(me == q)
                    def _():
                        back[q - off] = res[q]

    def collect(res, back, bs, br):
        for o in range(n_own):

            @pl.when(me != off + o)
            def _():
                from_owner(o, res, back, bs, br).wait_recv()

    def finish(send, recv, res, back, ss, rs_, bs, br):
        for o in range(n_own):

            @pl.when(me != off + o)
            def _():
                to_owner(o, send, recv, ss, rs_).wait_send()

        @pl.when(owner)
        def _():
            for q in range(n):

                @pl.when(me != q)
                def _():
                    to_peer(q, res, back, bs, br).wait_send()

    def slot(i):
        return i // tpo, slice((i % tpo) * SUB, (i % tpo + 1) * SUB)

    def pass_a(k, carry):
        trans, depth = carry
        new_trans, new_depth = [], []
        for i, (r, c) in enumerate(tiles):
            d = D[k + 1, rs(r), cs(c)]
            o = d * step
            p = jnp.exp(-o)
            op = 1.0 - p
            W[k, rs(r), cs(c)] = trans[i] * (op * d)
            U[k, rs(r), cs(c)] = trans[i] * ((op + o * p) * float(full))
            new_trans.append(trans[i] * p)
            new_depth.append(depth[i] + o)
        return new_trans, new_depth

    ones = [jnp.ones((SUB, LANE), jnp.float32) for _ in tiles]
    zeros = [jnp.zeros((SUB, LANE), jnp.float32) for _ in tiles]
    _, depth = lax.fori_loop(0, nd, pass_a, (ones, zeros))
    for i, _ in enumerate(tiles):
        o, s = slot(i)
        d_send[o, s, :] = depth[i]

    peers = (n - 1) + (mine > 0).astype(jnp.int32) + (mine < m - 1).astype(jnp.int32)
    pl.semaphore_wait(barrier, peers)

    side_plans = []
    for i in range(chunks):
        part = pl.ds(i * per, per)
        side_plans.append(
            [
                link(up, rows_out.at[0, part], yhi.at[part]),
                link(down, rows_out.at[1, part], ylo.at[part]),
            ]
        )
        start_all(side_plans[-1])
    layer_plan = [link(near, D.at[1], xhi), link(far, D.at[nd], xlo)]
    start_all(layer_plan)
    scatter(d_send, d_recv, d_ss, d_rs)

    for load in small:
        load.wait()
    for r, c in tiles:
        PJ[rs(r), cs(c)] = sum(cot[ch, rs(r), cs(c)] * tint[ch] for ch in range(3))

    lane = lax.broadcasted_iota(jnp.int32, (SUB, LANE), 1)
    sub = lax.broadcasted_iota(jnp.int32, (SUB, LANE), 0)
    first_lane, last_lane = lane == 0, lane == LANE - 1
    first_sub, last_sub = sub == 0, sub == SUB - 1

    def along_cols(row_of_tiles):
        ahead = [pltpu.roll(t, 1, 1) for t in row_of_tiles]
        after = [pltpu.roll(t, LANE - 1, 1) for t in row_of_tiles]
        prev = [jnp.where(first_lane, ahead[c - 1] if c else 0.0, ahead[c]) for c in range(nc)]
        nxt = [
            jnp.where(last_lane, after[c + 1] if c < nc - 1 else 0.0, after[c]) for c in range(nc)
        ]
        return prev, nxt

    def along_rows(col_of_tiles, above, below):
        down_ = [pltpu.roll(t, 1, 0) for t in col_of_tiles]
        up_ = [pltpu.roll(t, SUB - 1, 0) for t in col_of_tiles]
        prev = [jnp.where(first_sub, down_[r - 1] if r else above, down_[r]) for r in range(nr)]
        nxt = [jnp.where(last_sub, up_[r + 1] if r < nr - 1 else below, up_[r]) for r in range(nr)]
        return prev, nxt

    def wide(row):
        return jnp.broadcast_to(row, (SUB, LANE))

    half = [light[a] * 0.5 for a in range(3)]

    def before_rows(k, ahead, after):
        for r in range(nr):
            prev, nxt = along_cols([D[k + 1, rs(r), cs(c)] for c in range(nc)])
            for c in range(nc):
                at = (k, rs(r), cs(c))
                dx = after[k + 2, rs(r), cs(c)] - ahead[k, rs(r), cs(c)]
                dz = nxt[c] - prev[c]
                DX[at] = dx
                DZ[at] = dz
                INV[at] = 1.0 + 0.25 * (dx * dx + dz * dz)
                Q[at] = half[0] * dx + half[2] * dz

    def pass_b0(k, carry):
        before_rows(k, D, D)
        return carry

    def pass_b(k, total, at_first=False):
        new = []
        for c in range(nc):
            prev, nxt = along_rows(
                [D[k + 1, rs(r), cs(c)] for r in range(nr)],
                wide(ylo[k, :, cs(c)]),
                wide(yhi[k, :, cs(c)]),
            )
            for r in range(nr):
                at = (k, rs(r), cs(c))
                dy = nxt[r] - prev[r]
                inv = lax.rsqrt(INV[at] + 0.25 * (dy * dy))
                q = (Q[at] + half[1] * dy) * inv
                here_now = W[at] * (0.5 + 0.5 * q)
                now = total[len(new)] + here_now
                DY[at] = dy
                INV[at] = inv
                Q[at] = q
                if at_first:
                    E0[rs(r), cs(c)] = here_now
                    CUM[at] = jnp.zeros((SUB, LANE), jnp.float32)
                else:
                    CUM[at] = now
                new.append(now)
        return new

    lax.fori_loop(1, nd - 1, pass_b0, 0)

    def fronts():
        acc = jnp.zeros(d_recv.shape[1:], jnp.float32)
        for q in range(n):
            d_res[q] = jnp.exp(-acc)
            acc = acc + d_recv[q]

    emitted = zeros
    for i in range(chunks):
        arrive(side_plans[i])
        lo = max(i * per, 1)
        hi = min((i + 1) * per, nd - 1)
        if i == chunks - 1:
            combine(d_send, d_recv, d_res, d_back, d_ss, d_rs, d_bs, d_br, fronts)
        emitted = lax.fori_loop(lo, hi, pass_b, emitted)
    arrive(layer_plan)
    for r, c in tiles:
        D[0, rs(r), cs(c)] = xlo[rs(r), cs(c)]
        D[nd + 1, rs(r), cs(c)] = xhi[rs(r), cs(c)]
    before_rows(0, D, D)
    before_rows(nd - 1, D, D)
    emitted = pass_b(nd - 1, emitted)
    emitted = pass_b(0, emitted, True)
    for i, (r, c) in enumerate(tiles):
        o, s = slot(i)
        v_send[o, s, :] = PJ[rs(r), cs(c)] * emitted[i]
    scatter(v_send, v_recv, v_ss, v_rs)

    def pass_c(k, carry):
        for c in range(nc):
            for r in range(nr):
                at = (k, rs(r), cs(c))
                inv = INV[at]
                s = (PJ[rs(r), cs(c)] * (0.25 * full)) * W[at] * inv
                b = s * (Q[at] * inv) * 0.5
                AX[k + 1, rs(r), cs(c)] = s * light[0] - b * DX[at]
                ay = s * light[1] - b * DY[at]
                DY[at] = ay
                DZ[at] = s * light[2] - b * DZ[at]
                if r == 0:
                    edge_out[0, k, :, cs(c)] = ay[0:1]
                if r == nr - 1:
                    edge_out[1, k, :, cs(c)] = ay[SUB - 1 : SUB]
        return carry

    lax.fori_loop(0, nd, pass_c, 0)
    for i, (r, c) in enumerate(tiles):
        o, s = slot(i)
        axsend[rs(r), cs(c)] = AX[nd, rs(r), cs(c)] * jnp.exp(d_send[o, s, :])
    adj_plan = [
        link(up, edge_out.at[0], ayhi),
        link(down, edge_out.at[1], aylo),
        link(near, AX.at[1], axhi),
        link(far, axsend, axlo),
    ]
    start_all(adj_plan)

    def beyond():
        acc = jnp.zeros(v_recv.shape[1:], jnp.float32)
        for q in reversed(range(n)):
            acc = acc + d_res[q] * v_recv[q]
            v_res[q] = acc * EXTINCTION

    def value_combine():
        combine(v_send, v_recv, v_res, v_back, v_ss, v_rs, v_bs, v_br, beyond)

    def before_front(k, carry):
        for r, c in tiles:
            at = (k, rs(r), cs(c))
            own = PJ[rs(r), cs(c)] * (U[at] * (0.5 + 0.5 * Q[at]) + EXTINCTION * CUM[at])
            U[at] = own + (AX[k, rs(r), cs(c)] - AX[k + 2, rs(r), cs(c)])
        return carry

    lax.fori_loop(1, nd - 1, before_front, 0)

    collect(d_res, d_back, d_bs, d_br)
    for i, (r, c) in enumerate(tiles):
        o, s = slot(i)
        FR[rs(r), cs(c)] = d_back[o, s, :]
    front_out[0] = FR[0:1, :]
    front_out[1] = FR[rows - 1 : rows, :]
    front_plan = [link(up, front_out.at[0], fhi), link(down, front_out.at[1], flo)]
    start_all(front_plan)
    value_combine()

    def pass_d(k, carry):
        fr = {(r, c): FR[rs(r), cs(c)] for r, c in tiles}
        z = [
            along_cols([fr[r, c] * DZ[k, rs(r), cs(c)] for c in range(nc)]) for r in range(nr)
        ]
        for c in range(nc):
            prev, nxt = along_rows(
                [fr[r, c] * DY[k, rs(r), cs(c)] for r in range(nr)], 0.0, 0.0
            )
            for r in range(nr):
                at = (k, rs(r), cs(c))
                FA[at] = fr[r, c] * U[at] + (prev[r] - nxt[r]) + (z[r][0][c] - z[r][1][c])
        return carry

    lax.fori_loop(1, nd - 1, pass_d, 0)
    arrive(adj_plan)
    for i, (r, c) in enumerate(tiles):
        o, s = slot(i)
        AX[0, rs(r), cs(c)] = axlo[rs(r), cs(c)]
        AX[nd + 1, rs(r), cs(c)] = axhi[rs(r), cs(c)] * jnp.exp(-d_send[o, s, :])
    def ends(i, carry):
        k = i * (nd - 1)
        before_front(k, carry)
        return pass_d(k, carry)

    lax.fori_loop(0, 2, ends, 0)
    arrive(front_plan)

    def pass_e(k, carry):
        for c in range(nc):
            top = wide(flo[:, cs(c)] * aylo[k, :, cs(c)])
            at = (k, rs(0), cs(c))
            FA[at] = FA[at] + jnp.where(first_sub, top, 0.0)
            bottom = wide(fhi[:, cs(c)] * ayhi[k, :, cs(c)])
            at = (k, rs(nr - 1), cs(c))
            FA[at] = FA[at] - jnp.where(last_sub, bottom, 0.0)
        return carry

    lax.fori_loop(0, nd, pass_e, 0)

    collect(v_res, v_back, v_bs, v_br)
    for i, (r, c) in enumerate(tiles):
        o, s = slot(i)
        at = (rs(r), cs(c))
        e_out[at] = v_back[o, s, :] - EXTINCTION * (FR[at] * (PJ[at] * E0[at]))
    for sends, _, copy, _ in every:
        pl.when(sends)(copy.wait_send)
    finish(d_send, d_recv, d_res, d_back, d_ss, d_rs, d_bs, d_br)
    finish(v_send, v_recv, v_res, v_back, v_ss, v_rs, v_bs, v_br)


def local(n, m, density, light_dir, colour_tint, cotangent):
    nd, rows, cols = density.shape
    tiles = (rows // SUB) * (cols // LANE)
    n_own = owners_of(tiles, max(n // 2, 1))
    off = (n - n_own) // 2
    chunk = (tiles // n_own * SUB, LANE)
    chunks = 4 if nd % 4 == 0 else 1
    f32 = jnp.float32

    def vmem(*shape):
        return pltpu.VMEM(shape, f32)

    dma = pltpu.SemaphoreType.DMA
    volume = vmem(nd, rows, cols)
    padded = vmem(nd + 2, rows, cols)
    layer = vmem(rows, cols)
    side = vmem(nd, 1, cols)
    scan = [
        vmem(n_own, *chunk),
        vmem(n, *chunk),
        vmem(n, *chunk),
        vmem(n_own, *chunk),
    ]
    scan_sems = [dma((n_own,)), dma((n,)), dma((n,)), dma((n_own,))]
    links = 2 * chunks + 8
    scratch = (
        [pltpu.SMEM(light_dir.shape, f32), pltpu.SMEM(colour_tint.shape, f32)]
        + [vmem(*cotangent.shape), padded]
        + [volume] * 8
        + [padded]
        + [layer] * 3
        + [layer] * 5
        + [vmem(2, nd, 1, cols), side, side]
        + [vmem(2, nd, 1, cols), side, side]
        + [vmem(2, 1, cols), vmem(1, cols), vmem(1, cols)]
        + scan
        + scan
        + [dma((chunks,)), dma((3,)), dma((links,)), dma((links,))]
        + scan_sems
        + scan_sems
    )
    hbm = pl.BlockSpec(memory_space=pltpu.HBM)
    fa, e = pl.pallas_call(
        functools.partial(kernel, n, m, off),
        out_shape=(
            jax.ShapeDtypeStruct((nd, rows, cols), f32),
            jax.ShapeDtypeStruct((rows, cols), f32),
        ),
        in_specs=[hbm, hbm, hbm, hbm],
        out_specs=(
            pl.BlockSpec(memory_space=pltpu.VMEM),
            pl.BlockSpec(memory_space=pltpu.VMEM),
        ),
        scratch_shapes=scratch,
        compiler_params=pltpu.CompilerParams(
            collective_id=0, has_side_effects=True, vmem_limit_bytes=53_500_000
        ),
        name="render_grad",
    )(light_dir, colour_tint, cotangent, density)
    return fa - e[None]


def solution(mesh):
    placed = (P("ray", "row", None), P(), P(), P(None, "row", None))
    return jax.shard_map(
        functools.partial(local, mesh.shape["ray"], mesh.shape["row"]),
        mesh=mesh,
        in_specs=placed,
        out_specs=P("ray", "row", None),
        check_vma=False,
    )
```

```python
import functools

import jax
import jax.numpy as jnp
from jax import lax
from jax.experimental import pallas as pl
from jax.experimental.pallas import tpu as pltpu
from jax.sharding import PartitionSpec as P

EXTINCTION = 0.7
SUB = 8
LANE = 128
MESH = pl.DeviceIdType.MESH


def owners_of(tiles, n):
    own = min(n, tiles)
    while tiles % own:
        own -= 1
    return own


def kernel(
    n,
    m,
    off,
    light_hbm,
    tint_hbm,
    cot_hbm,
    dens_hbm,
    FA,
    e_out,
    light,
    tint,
    cot,
    D,
    W,
    U,
    INV,
    Q,
    DX,
    DY,
    DZ,
    CUM,
    AX,
    PJ,
    FR,
    FL,
    FN,
    E0,
    xlo,
    xhi,
    axlo,
    axhi,
    axsend,
    rows_out,
    ylo,
    yhi,
    edge_out,
    aylo,
    ayhi,
    front_out,
    flo,
    fhi,
    d_send,
    d_recv,
    d_res,
    d_back,
    v_send,
    v_recv,
    v_res,
    v_back,
    in_sem,
    small_sem,
    halo_ss,
    halo_rs,
    d_ss,
    d_rs,
    d_bs,
    d_br,
    v_ss,
    v_rs,
    v_bs,
    v_br,
):
    me = lax.axis_index("ray")
    mine = lax.axis_index("row")
    nd, rows, cols = dens_hbm.shape
    nr, nc = rows // SUB, cols // LANE
    full = nd * n
    step = EXTINCTION / full
    n_own = v_send.shape[0]
    tpo = nr * nc // n_own
    tiles = [(r, c) for c in range(nc) for r in range(nr)]
    chunks = in_sem.shape[0]
    per = nd // chunks

    def rs(r):
        return slice(r * SUB, (r + 1) * SUB)

    def cs(c):
        return slice(c * LANE, (c + 1) * LANE)

    barrier = pltpu.get_barrier_semaphore()
    for q in range(n):

        @pl.when(me != q)
        def _():
            pl.semaphore_signal(barrier, inc=1, device_id={"ray": q}, device_id_type=MESH)

    @pl.when(mine > 0)
    def _():
        pl.semaphore_signal(barrier, inc=1, device_id={"row": mine - 1}, device_id_type=MESH)

    @pl.when(mine < m - 1)
    def _():
        pl.semaphore_signal(barrier, inc=1, device_id={"row": mine + 1}, device_id_type=MESH)

    loads = [
        pltpu.make_async_copy(
            dens_hbm.at[pl.ds(i * per, per)], D.at[pl.ds(1 + i * per, per)], in_sem.at[i]
        )
        for i in range(chunks)
    ]
    small = [
        pltpu.make_async_copy(light_hbm, light, small_sem.at[0]),
        pltpu.make_async_copy(tint_hbm, tint, small_sem.at[1]),
        pltpu.make_async_copy(cot_hbm, cot, small_sem.at[2]),
    ]
    for load in loads + small:
        load.start()
    for i, load in enumerate(loads):
        load.wait()
        for k in range(i * per, (i + 1) * per):
            rows_out[0, k] = D[1 + k, 0:1, :]
            rows_out[1, k] = D[1 + k, rows - 1 : rows, :]

    used = [0]

    def link(to, src, dst):
        axis, by = to
        here, last = (mine, m - 1) if axis == "row" else (me, n - 1)
        if by < 0:
            sends, receives, where = here > 0, here < last, jnp.maximum(here - 1, 0)
        else:
            sends, receives, where = here < last, here > 0, jnp.minimum(here + 1, last)
        i = used[0]
        used[0] += 1
        copy = pltpu.make_async_remote_copy(
            src_ref=src,
            dst_ref=dst,
            send_sem=halo_ss.at[i],
            recv_sem=halo_rs.at[i],
            device_id={axis: where},
            device_id_type=MESH,
        )
        return sends, receives, copy, dst

    up, down, near, far = ("row", -1), ("row", 1), ("ray", -1), ("ray", 1)
    every = []

    def start_all(plan):
        every.extend(plan)
        for sends, _, copy, _ in plan:
            pl.when(sends)(copy.start)

    def arrive(plan):
        for _, receives, copy, dst in plan:
            pl.when(receives)(copy.wait_recv)

            @pl.when(jnp.logical_not(receives))
            def _():
                dst[...] = jnp.zeros(dst.shape, jnp.float32)

    def to_owner(o, send, recv, ss, rs_):
        return pltpu.make_async_remote_copy(
            src_ref=send.at[o],
            dst_ref=recv.at[me],
            send_sem=ss.at[o],
            recv_sem=rs_.at[me],
            device_id={"ray": off + o},
            device_id_type=MESH,
        )

    def from_peer(q, send, recv, ss, rs_):
        return pltpu.make_async_remote_copy(
            src_ref=send.at[0],
            dst_ref=recv.at[q],
            send_sem=ss.at[0],
            recv_sem=rs_.at[q],
            device_id={"ray": q},
            device_id_type=MESH,
        )

    def to_peer(q, res, back, bs, br):
        mine_as_owner = jnp.clip(me - off, 0, n_own - 1)
        return pltpu.make_async_remote_copy(
            src_ref=res.at[q],
            dst_ref=back.at[mine_as_owner],
            send_sem=bs.at[q],
            recv_sem=br.at[mine_as_owner],
            device_id={"ray": q},
            device_id_type=MESH,
        )

    def from_owner(o, res, back, bs, br):
        return pltpu.make_async_remote_copy(
            src_ref=res.at[0],
            dst_ref=back.at[o],
            send_sem=bs.at[0],
            recv_sem=br.at[o],
            device_id={"ray": off + o},
            device_id_type=MESH,
        )

    owner = jnp.logical_and(me >= off, me < off + n_own)

    def scatter(send, recv, ss, rs_):
        for o in range(n_own):

            @pl.when(me != off + o)
            def _():
                to_owner(o, send, recv, ss, rs_).start()

            @pl.when(me == off + o)
            def _():
                recv[off + o] = send[o]

    def combine(send, recv, res, back, ss, rs_, bs, br, total):
        @pl.when(owner)
        def _():
            for q in range(n):

                @pl.when(me != q)
                def _():
                    from_peer(q, send, recv, ss, rs_).wait_recv()

            total()
            for q in range(n):

                @pl.when(me != q)
                def _():
                    to_peer(q, res, back, bs, br).start()

                if off <= q < off + n_own:

                    @pl.when(me == q)
                    def _():
                        back[q - off] = res[q]

    def collect(res, back, bs, br):
        for o in range(n_own):

            @pl.when(me != off + o)
            def _():
                from_owner(o, res, back, bs, br).wait_recv()

    def finish(send, recv, res, back, ss, rs_, bs, br):
        for o in range(n_own):

            @pl.when(me != off + o)
            def _():
                to_owner(o, send, recv, ss, rs_).wait_send()

        @pl.when(owner)
        def _():
            for q in range(n):

                @pl.when(me != q)
                def _():
                    to_peer(q, res, back, bs, br).wait_send()

    def slot(i):
        return i // tpo, slice((i % tpo) * SUB, (i % tpo + 1) * SUB)

    for load in small:
        load.wait()
    for r, c in tiles:
        PJ[rs(r), cs(c)] = sum(cot[ch, rs(r), cs(c)] * tint[ch] for ch in range(3))

    lane = lax.broadcasted_iota(jnp.int32, (SUB, LANE), 1)
    sub = lax.broadcasted_iota(jnp.int32, (SUB, LANE), 0)
    first_lane, last_lane = lane == 0, lane == LANE - 1
    first_sub, last_sub = sub == 0, sub == SUB - 1

    def along_cols(row_of_tiles):
        ahead = [pltpu.roll(t, 1, 1) for t in row_of_tiles]
        after = [pltpu.roll(t, LANE - 1, 1) for t in row_of_tiles]
        prev = [jnp.where(first_lane, ahead[c - 1] if c else 0.0, ahead[c]) for c in range(nc)]
        nxt = [
            jnp.where(last_lane, after[c + 1] if c < nc - 1 else 0.0, after[c]) for c in range(nc)
        ]
        return prev, nxt

    def along_rows(col_of_tiles, above, below):
        down_ = [pltpu.roll(t, 1, 0) for t in col_of_tiles]
        up_ = [pltpu.roll(t, SUB - 1, 0) for t in col_of_tiles]
        prev = [jnp.where(first_sub, down_[r - 1] if r else above, down_[r]) for r in range(nr)]
        nxt = [jnp.where(last_sub, up_[r + 1] if r < nr - 1 else below, up_[r]) for r in range(nr)]
        return prev, nxt

    def wide(row):
        return jnp.broadcast_to(row, (SUB, LANE))

    half = [light[a] * 0.5 for a in range(3)]

    def before_rows(k, ahead, after):
        for r in range(nr):
            prev, nxt = along_cols([D[k + 1, rs(r), cs(c)] for c in range(nc)])
            for c in range(nc):
                at = (k, rs(r), cs(c))
                dx = after[k + 2, rs(r), cs(c)] - ahead[k, rs(r), cs(c)]
                dz = nxt[c] - prev[c]
                DX[at] = dx
                DZ[at] = dz
                INV[at] = 1.0 + 0.25 * (dx * dx + dz * dz)
                Q[at] = half[0] * dx + half[2] * dz

    def pass_a(k, carry):
        trans, depth = carry
        new_trans, new_depth = [], []
        for i, (r, c) in enumerate(tiles):
            d = D[k + 1, rs(r), cs(c)]
            o = d * step
            p = jnp.exp(-o)
            op = 1.0 - p
            W[k, rs(r), cs(c)] = trans[i] * (op * d)
            U[k, rs(r), cs(c)] = trans[i] * ((op + o * p) * float(full))
            new_trans.append(trans[i] * p)
            new_depth.append(depth[i] + o)
        before_rows(k, D, D)
        return new_trans, new_depth

    ones = [jnp.ones((SUB, LANE), jnp.float32) for _ in tiles]
    zeros = [jnp.zeros((SUB, LANE), jnp.float32) for _ in tiles]
    for r, c in tiles:
        D[0, rs(r), cs(c)] = zeros[0]
        D[nd + 1, rs(r), cs(c)] = zeros[0]
    state = lax.fori_loop(0, nd // 2, pass_a, (ones, zeros))

    peers = (n - 1) + (mine > 0).astype(jnp.int32) + (mine < m - 1).astype(jnp.int32)
    pl.semaphore_wait(barrier, peers)

    side_plans = []
    for i in range(chunks):
        part = pl.ds(i * per, per)
        side_plans.append(
            [
                link(up, rows_out.at[0, part], yhi.at[part]),
                link(down, rows_out.at[1, part], ylo.at[part]),
            ]
        )
        start_all(side_plans[-1])
    layer_plan = [link(near, D.at[1], xhi), link(far, D.at[nd], xlo)]
    start_all(layer_plan)
    _, depth = lax.fori_loop(nd // 2, nd, pass_a, state)
    for i, _ in enumerate(tiles):
        o, s = slot(i)
        d_send[o, s, :] = depth[i]
    scatter(d_send, d_recv, d_ss, d_rs)

    def pass_b(k, total, at_first=False):
        new = []
        for c in range(nc):
            prev, nxt = along_rows(
                [D[k + 1, rs(r), cs(c)] for r in range(nr)],
                wide(ylo[k, :, cs(c)]),
                wide(yhi[k, :, cs(c)]),
            )
            for r in range(nr):
                at = (k, rs(r), cs(c))
                dy = nxt[r] - prev[r]
                inv = lax.rsqrt(INV[at] + 0.25 * (dy * dy))
                q = (Q[at] + half[1] * dy) * inv
                here_now = W[at] * (0.5 + 0.5 * q)
                now = total[len(new)] + here_now
                DY[at] = dy
                INV[at] = inv
                Q[at] = q
                if at_first:
                    E0[rs(r), cs(c)] = here_now
                    CUM[at] = jnp.zeros((SUB, LANE), jnp.float32)
                else:
                    CUM[at] = now
                new.append(now)
        return new

    def fronts():
        acc = jnp.zeros(d_recv.shape[1:], jnp.float32)
        for q in range(n):
            d_res[q] = jnp.exp(-acc)
            acc = acc + d_recv[q]

    emitted = zeros
    for i in range(chunks):
        arrive(side_plans[i])
        lo = max(i * per, 1)
        hi = min((i + 1) * per, nd - 1)
        emitted = lax.fori_loop(lo, hi, pass_b, emitted)
    arrive(layer_plan)
    for r, c in tiles:
        D[0, rs(r), cs(c)] = xlo[rs(r), cs(c)]
        D[nd + 1, rs(r), cs(c)] = xhi[rs(r), cs(c)]
    before_rows(0, D, D)
    before_rows(nd - 1, D, D)
    emitted = pass_b(nd - 1, emitted)
    emitted = pass_b(0, emitted, True)
    for i, (r, c) in enumerate(tiles):
        o, s = slot(i)
        v_send[o, s, :] = PJ[rs(r), cs(c)] * emitted[i]
    scatter(v_send, v_recv, v_ss, v_rs)

    def pass_c(k, carry):
        for r in range(nr):
            az = []
            for c in range(nc):
                at = (k, rs(r), cs(c))
                inv = INV[at]
                s = (PJ[rs(r), cs(c)] * (0.25 * full)) * W[at] * inv
                b = s * (Q[at] * inv) * 0.5
                AX[k + 1, rs(r), cs(c)] = s * light[0] - b * DX[at]
                ay = s * light[1] - b * DY[at]
                DY[at] = ay
                az.append(s * light[2] - b * DZ[at])
                if r == 0:
                    edge_out[0, k, :, cs(c)] = ay[0:1]
                if r == nr - 1:
                    edge_out[1, k, :, cs(c)] = ay[SUB - 1 : SUB]
            prev, nxt = along_cols(az)
            for c in range(nc):
                DZ[k, rs(r), cs(c)] = prev[c]
                DX[k, rs(r), cs(c)] = nxt[c]
        return carry

    cut = nd // 2
    lax.fori_loop(0, cut, pass_c, 0)
    combine(d_send, d_recv, d_res, d_back, d_ss, d_rs, d_bs, d_br, fronts)
    lax.fori_loop(cut, nd, pass_c, 0)
    for i, (r, c) in enumerate(tiles):
        o, s = slot(i)
        axsend[rs(r), cs(c)] = AX[nd, rs(r), cs(c)] * jnp.exp(d_send[o, s, :])
    adj_plan = [
        link(up, edge_out.at[0], ayhi),
        link(down, edge_out.at[1], aylo),
        link(near, AX.at[1], axhi),
        link(far, axsend, axlo),
    ]
    start_all(adj_plan)

    def beyond():
        acc = jnp.zeros(v_recv.shape[1:], jnp.float32)
        for q in reversed(range(n)):
            acc = acc + d_res[q] * v_recv[q]
            v_res[q] = acc * EXTINCTION

    def value_combine():
        combine(v_send, v_recv, v_res, v_back, v_ss, v_rs, v_bs, v_br, beyond)

    def before_front(k, carry):
        for r, c in tiles:
            at = (k, rs(r), cs(c))
            own = PJ[rs(r), cs(c)] * (U[at] * (0.5 + 0.5 * Q[at]) + EXTINCTION * CUM[at])
            U[at] = own + (AX[k, rs(r), cs(c)] - AX[k + 2, rs(r), cs(c)])
        return carry

    lax.fori_loop(1, nd - 1, before_front, 0)

    collect(d_res, d_back, d_bs, d_br)
    for i, (r, c) in enumerate(tiles):
        o, s = slot(i)
        FR[rs(r), cs(c)] = d_back[o, s, :]
    for r in range(nr):
        prev, nxt = along_cols([FR[rs(r), cs(c)] for c in range(nc)])
        for c in range(nc):
            FL[rs(r), cs(c)] = prev[c]
            FN[rs(r), cs(c)] = nxt[c]
    front_out[0] = FR[0:1, :]
    front_out[1] = FR[rows - 1 : rows, :]
    front_plan = [link(up, front_out.at[0], fhi), link(down, front_out.at[1], flo)]
    start_all(front_plan)
    value_combine()

    def pass_d(k, carry):
        fr = {(r, c): FR[rs(r), cs(c)] for r, c in tiles}
        for c in range(nc):
            prev, nxt = along_rows(
                [fr[r, c] * DY[k, rs(r), cs(c)] for r in range(nr)], 0.0, 0.0
            )
            for r in range(nr):
                at = (k, rs(r), cs(c))
                fz = FL[rs(r), cs(c)] * DZ[at] - FN[rs(r), cs(c)] * DX[at]
                FA[at] = fr[r, c] * U[at] + (prev[r] - nxt[r]) + fz
        return carry

    lax.fori_loop(1, nd - 1, pass_d, 0)
    arrive(adj_plan)
    for i, (r, c) in enumerate(tiles):
        o, s = slot(i)
        AX[0, rs(r), cs(c)] = axlo[rs(r), cs(c)]
        AX[nd + 1, rs(r), cs(c)] = axhi[rs(r), cs(c)] * jnp.exp(-d_send[o, s, :])
    def ends(i, carry):
        k = i * (nd - 1)
        before_front(k, carry)
        return pass_d(k, carry)

    lax.fori_loop(0, 2, ends, 0)
    arrive(front_plan)

    def pass_e(k, carry):
        for c in range(nc):
            top = wide(flo[:, cs(c)] * aylo[k, :, cs(c)])
            at = (k, rs(0), cs(c))
            FA[at] = FA[at] + jnp.where(first_sub, top, 0.0)
            bottom = wide(fhi[:, cs(c)] * ayhi[k, :, cs(c)])
            at = (k, rs(nr - 1), cs(c))
            FA[at] = FA[at] - jnp.where(last_sub, bottom, 0.0)
        return carry

    lax.fori_loop(0, nd, pass_e, 0)

    collect(v_res, v_back, v_bs, v_br)
    for i, (r, c) in enumerate(tiles):
        o, s = slot(i)
        at = (rs(r), cs(c))
        e_out[at] = v_back[o, s, :] - EXTINCTION * (FR[at] * (PJ[at] * E0[at]))
    for sends, _, copy, _ in every:
        pl.when(sends)(copy.wait_send)
    finish(d_send, d_recv, d_res, d_back, d_ss, d_rs, d_bs, d_br)
    finish(v_send, v_recv, v_res, v_back, v_ss, v_rs, v_bs, v_br)


def local(n, m, density, light_dir, colour_tint, cotangent):
    nd, rows, cols = density.shape
    tiles = (rows // SUB) * (cols // LANE)
    n_own = owners_of(tiles, max(n // 2, 1))
    off = (n - n_own) // 2
    chunk = (tiles // n_own * SUB, LANE)
    chunks = 4 if nd % 4 == 0 else 1
    f32 = jnp.float32

    def vmem(*shape):
        return pltpu.VMEM(shape, f32)

    dma = pltpu.SemaphoreType.DMA
    volume = vmem(nd, rows, cols)
    padded = vmem(nd + 2, rows, cols)
    layer = vmem(rows, cols)
    side = vmem(nd, 1, cols)
    scan = [
        vmem(n_own, *chunk),
        vmem(n, *chunk),
        vmem(n, *chunk),
        vmem(n_own, *chunk),
    ]
    scan_sems = [dma((n_own,)), dma((n,)), dma((n,)), dma((n_own,))]
    links = 2 * chunks + 8
    scratch = (
        [pltpu.SMEM(light_dir.shape, f32), pltpu.SMEM(colour_tint.shape, f32)]
        + [vmem(*cotangent.shape), padded]
        + [volume] * 8
        + [padded]
        + [layer] * 5
        + [layer] * 5
        + [vmem(2, nd, 1, cols), side, side]
        + [vmem(2, nd, 1, cols), side, side]
        + [vmem(2, 1, cols), vmem(1, cols), vmem(1, cols)]
        + scan
        + scan
        + [dma((chunks,)), dma((3,)), dma((links,)), dma((links,))]
        + scan_sems
        + scan_sems
    )
    hbm = pl.BlockSpec(memory_space=pltpu.HBM)
    fa, e = pl.pallas_call(
        functools.partial(kernel, n, m, off),
        out_shape=(
            jax.ShapeDtypeStruct((nd, rows, cols), f32),
            jax.ShapeDtypeStruct((rows, cols), f32),
        ),
        in_specs=[hbm, hbm, hbm, hbm],
        out_specs=(
            pl.BlockSpec(memory_space=pltpu.VMEM),
            pl.BlockSpec(memory_space=pltpu.VMEM),
        ),
        scratch_shapes=scratch,
        compiler_params=pltpu.CompilerParams(
            collective_id=0, has_side_effects=True, vmem_limit_bytes=53_500_000
        ),
        name="render_grad",
    )(light_dir, colour_tint, cotangent, density)
    return fa - e[None]


def solution(mesh):
    placed = (P("ray", "row", None), P(), P(), P(None, "row", None))
    return jax.shard_map(
        functools.partial(local, mesh.shape["ray"], mesh.shape["row"]),
        mesh=mesh,
        in_specs=placed,
        out_specs=P("ray", "row", None),
        check_vma=False,
    )
```

```python
import functools

import jax
import jax.numpy as jnp
from jax import lax
from jax.experimental import pallas as pl
from jax.experimental.pallas import tpu as pltpu
from jax.sharding import PartitionSpec as P

EXTINCTION = 0.7
SUB = 8
LANE = 128
MESH = pl.DeviceIdType.MESH


def owners_of(tiles, n):
    own = min(n, tiles)
    while tiles % own:
        own -= 1
    return own


def kernel(
    n,
    m,
    off,
    light_hbm,
    tint_hbm,
    cot_hbm,
    dens_hbm,
    FA,
    e_out,
    light,
    tint,
    cot,
    D,
    W,
    U,
    INV,
    Q,
    DX,
    DY,
    DZ,
    CUM,
    AX,
    PJ,
    FR,
    FL,
    FN,
    E0,
    xlo,
    xhi,
    axlo,
    axhi,
    axsend,
    rows_out,
    ylo,
    yhi,
    edge_out,
    aylo,
    ayhi,
    front_out,
    flo,
    fhi,
    d_send,
    d_recv,
    d_res,
    d_back,
    v_send,
    v_recv,
    v_res,
    v_back,
    in_sem,
    small_sem,
    halo_ss,
    halo_rs,
    d_ss,
    d_rs,
    d_bs,
    d_br,
    v_ss,
    v_rs,
    v_bs,
    v_br,
):
    me = lax.axis_index("ray")
    mine = lax.axis_index("row")
    nd, rows, cols = dens_hbm.shape
    nr, nc = rows // SUB, cols // LANE
    full = nd * n
    step = EXTINCTION / full
    n_own = v_send.shape[0]
    tpo = nr * nc // n_own
    tiles = [(r, c) for c in range(nc) for r in range(nr)]
    chunks = in_sem.shape[0]
    per = nd // chunks

    def rs(r):
        return slice(r * SUB, (r + 1) * SUB)

    def cs(c):
        return slice(c * LANE, (c + 1) * LANE)

    barrier = pltpu.get_barrier_semaphore()
    for q in range(n):

        @pl.when(me != q)
        def _():
            pl.semaphore_signal(barrier, inc=1, device_id={"ray": q}, device_id_type=MESH)

    @pl.when(mine > 0)
    def _():
        pl.semaphore_signal(barrier, inc=1, device_id={"row": mine - 1}, device_id_type=MESH)

    @pl.when(mine < m - 1)
    def _():
        pl.semaphore_signal(barrier, inc=1, device_id={"row": mine + 1}, device_id_type=MESH)

    loads = [
        pltpu.make_async_copy(
            dens_hbm.at[pl.ds(i * per, per)], D.at[pl.ds(1 + i * per, per)], in_sem.at[i]
        )
        for i in range(chunks)
    ]
    small = [
        pltpu.make_async_copy(light_hbm, light, small_sem.at[0]),
        pltpu.make_async_copy(tint_hbm, tint, small_sem.at[1]),
        pltpu.make_async_copy(cot_hbm, cot, small_sem.at[2]),
    ]
    for load in loads + small:
        load.start()
    for i, load in enumerate(loads):
        load.wait()
        for k in range(i * per, (i + 1) * per):
            rows_out[0, k] = D[1 + k, 0:1, :]
            rows_out[1, k] = D[1 + k, rows - 1 : rows, :]

    used = [0]

    def link(to, src, dst):
        axis, by = to
        here, last = (mine, m - 1) if axis == "row" else (me, n - 1)
        if by < 0:
            sends, receives, where = here > 0, here < last, jnp.maximum(here - 1, 0)
        else:
            sends, receives, where = here < last, here > 0, jnp.minimum(here + 1, last)
        i = used[0]
        used[0] += 1
        copy = pltpu.make_async_remote_copy(
            src_ref=src,
            dst_ref=dst,
            send_sem=halo_ss.at[i],
            recv_sem=halo_rs.at[i],
            device_id={axis: where},
            device_id_type=MESH,
        )
        return sends, receives, copy, dst

    up, down, near, far = ("row", -1), ("row", 1), ("ray", -1), ("ray", 1)
    every = []

    def start_all(plan):
        every.extend(plan)
        for sends, _, copy, _ in plan:
            pl.when(sends)(copy.start)

    def arrive(plan):
        for _, receives, copy, dst in plan:
            pl.when(receives)(copy.wait_recv)

            @pl.when(jnp.logical_not(receives))
            def _():
                dst[...] = jnp.zeros(dst.shape, jnp.float32)

    def to_owner(o, send, recv, ss, rs_):
        return pltpu.make_async_remote_copy(
            src_ref=send.at[o],
            dst_ref=recv.at[me],
            send_sem=ss.at[o],
            recv_sem=rs_.at[me],
            device_id={"ray": off + o},
            device_id_type=MESH,
        )

    def from_peer(q, send, recv, ss, rs_):
        return pltpu.make_async_remote_copy(
            src_ref=send.at[0],
            dst_ref=recv.at[q],
            send_sem=ss.at[0],
            recv_sem=rs_.at[q],
            device_id={"ray": q},
            device_id_type=MESH,
        )

    def to_peer(q, res, back, bs, br):
        mine_as_owner = jnp.clip(me - off, 0, n_own - 1)
        return pltpu.make_async_remote_copy(
            src_ref=res.at[q],
            dst_ref=back.at[mine_as_owner],
            send_sem=bs.at[q],
            recv_sem=br.at[mine_as_owner],
            device_id={"ray": q},
            device_id_type=MESH,
        )

    def from_owner(o, res, back, bs, br):
        return pltpu.make_async_remote_copy(
            src_ref=res.at[0],
            dst_ref=back.at[o],
            send_sem=bs.at[0],
            recv_sem=br.at[o],
            device_id={"ray": off + o},
            device_id_type=MESH,
        )

    owner = jnp.logical_and(me >= off, me < off + n_own)

    def scatter(send, recv, ss, rs_):
        for o in range(n_own):

            @pl.when(me != off + o)
            def _():
                to_owner(o, send, recv, ss, rs_).start()

            @pl.when(me == off + o)
            def _():
                recv[off + o] = send[o]

    def combine(send, recv, res, back, ss, rs_, bs, br, total):
        @pl.when(owner)
        def _():
            for q in range(n):

                @pl.when(me != q)
                def _():
                    from_peer(q, send, recv, ss, rs_).wait_recv()

            total()
            for q in range(n):

                @pl.when(me != q)
                def _():
                    to_peer(q, res, back, bs, br).start()

                if off <= q < off + n_own:

                    @pl.when(me == q)
                    def _():
                        back[q - off] = res[q]

    def collect(res, back, bs, br):
        for o in range(n_own):

            @pl.when(me != off + o)
            def _():
                from_owner(o, res, back, bs, br).wait_recv()

    def finish(send, recv, res, back, ss, rs_, bs, br):
        for o in range(n_own):

            @pl.when(me != off + o)
            def _():
                to_owner(o, send, recv, ss, rs_).wait_send()

        @pl.when(owner)
        def _():
            for q in range(n):

                @pl.when(me != q)
                def _():
                    to_peer(q, res, back, bs, br).wait_send()

    def slot(i):
        return i // tpo, slice((i % tpo) * SUB, (i % tpo + 1) * SUB)

    for load in small:
        load.wait()
    for r, c in tiles:
        PJ[rs(r), cs(c)] = sum(cot[ch, rs(r), cs(c)] * tint[ch] for ch in range(3))

    lane = lax.broadcasted_iota(jnp.int32, (SUB, LANE), 1)
    sub = lax.broadcasted_iota(jnp.int32, (SUB, LANE), 0)
    first_lane, last_lane = lane == 0, lane == LANE - 1
    first_sub, last_sub = sub == 0, sub == SUB - 1

    def along_cols(row_of_tiles):
        ahead = [pltpu.roll(t, 1, 1) for t in row_of_tiles]
        after = [pltpu.roll(t, LANE - 1, 1) for t in row_of_tiles]
        prev = [jnp.where(first_lane, ahead[c - 1] if c else 0.0, ahead[c]) for c in range(nc)]
        nxt = [
            jnp.where(last_lane, after[c + 1] if c < nc - 1 else 0.0, after[c]) for c in range(nc)
        ]
        return prev, nxt

    def along_rows(col_of_tiles, above, below):
        down_ = [pltpu.roll(t, 1, 0) for t in col_of_tiles]
        up_ = [pltpu.roll(t, SUB - 1, 0) for t in col_of_tiles]
        prev = [jnp.where(first_sub, down_[r - 1] if r else above, down_[r]) for r in range(nr)]
        nxt = [jnp.where(last_sub, up_[r + 1] if r < nr - 1 else below, up_[r]) for r in range(nr)]
        return prev, nxt

    def wide(row):
        return jnp.broadcast_to(row, (SUB, LANE))

    half = [light[a] * 0.5 for a in range(3)]

    def before_rows(k, ahead, after):
        for r in range(nr):
            prev, nxt = along_cols([D[k + 1, rs(r), cs(c)] for c in range(nc)])
            for c in range(nc):
                at = (k, rs(r), cs(c))
                dx = after[k + 2, rs(r), cs(c)] - ahead[k, rs(r), cs(c)]
                dz = nxt[c] - prev[c]
                DX[at] = dx
                DZ[at] = dz
                INV[at] = 1.0 + 0.25 * (dx * dx + dz * dz)
                Q[at] = half[0] * dx + half[2] * dz

    def pass_a(k, carry, rows_too=True):
        trans, depth = carry
        new_trans, new_depth = [], []
        for i, (r, c) in enumerate(tiles):
            d = D[k + 1, rs(r), cs(c)]
            o = d * step
            p = jnp.exp(-o)
            op = 1.0 - p
            W[k, rs(r), cs(c)] = trans[i] * (op * d)
            U[k, rs(r), cs(c)] = trans[i] * ((op + o * p) * float(full))
            new_trans.append(trans[i] * p)
            new_depth.append(depth[i] + o)
        if rows_too:
            before_rows(k, D, D)
        return new_trans, new_depth

    ones = [jnp.ones((SUB, LANE), jnp.float32) for _ in tiles]
    zeros = [jnp.zeros((SUB, LANE), jnp.float32) for _ in tiles]
    for r, c in tiles:
        D[0, rs(r), cs(c)] = zeros[0]
        D[nd + 1, rs(r), cs(c)] = zeros[0]
    state = lax.fori_loop(0, nd // 2, pass_a, (ones, zeros))

    peers = (n - 1) + (mine > 0).astype(jnp.int32) + (mine < m - 1).astype(jnp.int32)
    pl.semaphore_wait(barrier, peers)

    side_plans = []
    for i in range(chunks):
        part = pl.ds(i * per, per)
        side_plans.append(
            [
                link(up, rows_out.at[0, part], yhi.at[part]),
                link(down, rows_out.at[1, part], ylo.at[part]),
            ]
        )
        start_all(side_plans[-1])
    layer_plan = [link(near, D.at[1], xhi), link(far, D.at[nd], xlo)]
    start_all(layer_plan)
    _, depth = lax.fori_loop(nd // 2, nd, functools.partial(pass_a, rows_too=False), state)
    for i, _ in enumerate(tiles):
        o, s = slot(i)
        d_send[o, s, :] = depth[i]
    scatter(d_send, d_recv, d_ss, d_rs)

    def pass_b0(k, carry):
        before_rows(k, D, D)
        return carry

    lax.fori_loop(nd // 2, nd, pass_b0, 0)

    def pass_b(k, total, at_first=False):
        new = []
        for c in range(nc):
            prev, nxt = along_rows(
                [D[k + 1, rs(r), cs(c)] for r in range(nr)],
                wide(ylo[k, :, cs(c)]),
                wide(yhi[k, :, cs(c)]),
            )
            for r in range(nr):
                at = (k, rs(r), cs(c))
                dy = nxt[r] - prev[r]
                inv = lax.rsqrt(INV[at] + 0.25 * (dy * dy))
                q = (Q[at] + half[1] * dy) * inv
                here_now = W[at] * (0.5 + 0.5 * q)
                now = total[len(new)] + here_now
                DY[at] = dy
                INV[at] = inv
                Q[at] = q
                if at_first:
                    E0[rs(r), cs(c)] = here_now
                    CUM[at] = jnp.zeros((SUB, LANE), jnp.float32)
                else:
                    CUM[at] = now
                new.append(now)
        return new

    def fronts():
        acc = jnp.zeros(d_recv.shape[1:], jnp.float32)
        for q in range(n):
            d_res[q] = jnp.exp(-acc)
            acc = acc + d_recv[q]

    emitted = zeros
    for i in range(chunks):
        arrive(side_plans[i])
        lo = max(i * per, 1)
        hi = min((i + 1) * per, nd - 1)
        emitted = lax.fori_loop(lo, hi, pass_b, emitted)
    arrive(layer_plan)
    for r, c in tiles:
        D[0, rs(r), cs(c)] = xlo[rs(r), cs(c)]
        D[nd + 1, rs(r), cs(c)] = xhi[rs(r), cs(c)]
    before_rows(0, D, D)
    before_rows(nd - 1, D, D)
    emitted = pass_b(nd - 1, emitted)
    emitted = pass_b(0, emitted, True)
    for i, (r, c) in enumerate(tiles):
        o, s = slot(i)
        v_send[o, s, :] = PJ[rs(r), cs(c)] * emitted[i]
    scatter(v_send, v_recv, v_ss, v_rs)

    def pass_c(k, carry):
        for r in range(nr):
            az = []
            for c in range(nc):
                at = (k, rs(r), cs(c))
                inv = INV[at]
                s = (PJ[rs(r), cs(c)] * (0.25 * full)) * W[at] * inv
                b = s * (Q[at] * inv) * 0.5
                AX[k + 1, rs(r), cs(c)] = s * light[0] - b * DX[at]
                ay = s * light[1] - b * DY[at]
                DY[at] = ay
                az.append(s * light[2] - b * DZ[at])
                if r == 0:
                    edge_out[0, k, :, cs(c)] = ay[0:1]
                if r == nr - 1:
                    edge_out[1, k, :, cs(c)] = ay[SUB - 1 : SUB]
            prev, nxt = along_cols(az)
            for c in range(nc):
                DZ[k, rs(r), cs(c)] = prev[c]
                DX[k, rs(r), cs(c)] = nxt[c]
        return carry

    cut = nd // 4
    lax.fori_loop(0, cut, pass_c, 0)
    combine(d_send, d_recv, d_res, d_back, d_ss, d_rs, d_bs, d_br, fronts)
    lax.fori_loop(cut, nd, pass_c, 0)
    for i, (r, c) in enumerate(tiles):
        o, s = slot(i)
        axsend[rs(r), cs(c)] = AX[nd, rs(r), cs(c)] * jnp.exp(d_send[o, s, :])
    adj_plan = [
        link(up, edge_out.at[0], ayhi),
        link(down, edge_out.at[1], aylo),
        link(near, AX.at[1], axhi),
        link(far, axsend, axlo),
    ]
    start_all(adj_plan)

    def beyond():
        acc = jnp.zeros(v_recv.shape[1:], jnp.float32)
        for q in reversed(range(n)):
            acc = acc + d_res[q] * v_recv[q]
            v_res[q] = acc * EXTINCTION

    def value_combine():
        combine(v_send, v_recv, v_res, v_back, v_ss, v_rs, v_bs, v_br, beyond)

    def before_front(k, carry):
        for r, c in tiles:
            at = (k, rs(r), cs(c))
            own = PJ[rs(r), cs(c)] * (U[at] * (0.5 + 0.5 * Q[at]) + EXTINCTION * CUM[at])
            U[at] = own + (AX[k, rs(r), cs(c)] - AX[k + 2, rs(r), cs(c)])
        return carry

    lax.fori_loop(1, nd - 1, before_front, 0)

    collect(d_res, d_back, d_bs, d_br)
    for i, (r, c) in enumerate(tiles):
        o, s = slot(i)
        FR[rs(r), cs(c)] = d_back[o, s, :]
    for r in range(nr):
        prev, nxt = along_cols([FR[rs(r), cs(c)] for c in range(nc)])
        for c in range(nc):
            FL[rs(r), cs(c)] = prev[c]
            FN[rs(r), cs(c)] = nxt[c]
    front_out[0] = FR[0:1, :]
    front_out[1] = FR[rows - 1 : rows, :]
    front_plan = [link(up, front_out.at[0], fhi), link(down, front_out.at[1], flo)]
    start_all(front_plan)
    value_combine()

    def pass_d(k, carry):
        fr = {(r, c): FR[rs(r), cs(c)] for r, c in tiles}
        for c in range(nc):
            prev, nxt = along_rows(
                [fr[r, c] * DY[k, rs(r), cs(c)] for r in range(nr)], 0.0, 0.0
            )
            for r in range(nr):
                at = (k, rs(r), cs(c))
                fz = FL[rs(r), cs(c)] * DZ[at] - FN[rs(r), cs(c)] * DX[at]
                FA[at] = fr[r, c] * U[at] + (prev[r] - nxt[r]) + fz
        return carry

    lax.fori_loop(1, nd - 1, pass_d, 0)
    arrive(adj_plan)
    for i, (r, c) in enumerate(tiles):
        o, s = slot(i)
        AX[0, rs(r), cs(c)] = axlo[rs(r), cs(c)]
        AX[nd + 1, rs(r), cs(c)] = axhi[rs(r), cs(c)] * jnp.exp(-d_send[o, s, :])
    def ends(i, carry):
        k = i * (nd - 1)
        before_front(k, carry)
        return pass_d(k, carry)

    lax.fori_loop(0, 2, ends, 0)
    arrive(front_plan)

    def pass_e(k, carry):
        for c in range(nc):
            top = wide(flo[:, cs(c)] * aylo[k, :, cs(c)])
            at = (k, rs(0), cs(c))
            FA[at] = FA[at] + jnp.where(first_sub, top, 0.0)
            bottom = wide(fhi[:, cs(c)] * ayhi[k, :, cs(c)])
            at = (k, rs(nr - 1), cs(c))
            FA[at] = FA[at] - jnp.where(last_sub, bottom, 0.0)
        return carry

    lax.fori_loop(0, nd, pass_e, 0)

    collect(v_res, v_back, v_bs, v_br)
    for i, (r, c) in enumerate(tiles):
        o, s = slot(i)
        at = (rs(r), cs(c))
        e_out[at] = v_back[o, s, :] - EXTINCTION * (FR[at] * (PJ[at] * E0[at]))
    for sends, _, copy, _ in every:
        pl.when(sends)(copy.wait_send)
    finish(d_send, d_recv, d_res, d_back, d_ss, d_rs, d_bs, d_br)
    finish(v_send, v_recv, v_res, v_back, v_ss, v_rs, v_bs, v_br)


def local(n, m, density, light_dir, colour_tint, cotangent):
    nd, rows, cols = density.shape
    tiles = (rows // SUB) * (cols // LANE)
    n_own = owners_of(tiles, max(n // 2, 1))
    off = (n - n_own) // 2
    chunk = (tiles // n_own * SUB, LANE)
    chunks = 4 if nd % 4 == 0 else 1
    f32 = jnp.float32

    def vmem(*shape):
        return pltpu.VMEM(shape, f32)

    dma = pltpu.SemaphoreType.DMA
    volume = vmem(nd, rows, cols)
    padded = vmem(nd + 2, rows, cols)
    layer = vmem(rows, cols)
    side = vmem(nd, 1, cols)
    scan = [
        vmem(n_own, *chunk),
        vmem(n, *chunk),
        vmem(n, *chunk),
        vmem(n_own, *chunk),
    ]
    scan_sems = [dma((n_own,)), dma((n,)), dma((n,)), dma((n_own,))]
    links = 2 * chunks + 8
    scratch = (
        [pltpu.SMEM(light_dir.shape, f32), pltpu.SMEM(colour_tint.shape, f32)]
        + [vmem(*cotangent.shape), padded]
        + [volume] * 8
        + [padded]
        + [layer] * 5
        + [layer] * 5
        + [vmem(2, nd, 1, cols), side, side]
        + [vmem(2, nd, 1, cols), side, side]
        + [vmem(2, 1, cols), vmem(1, cols), vmem(1, cols)]
        + scan
        + scan
        + [dma((chunks,)), dma((3,)), dma((links,)), dma((links,))]
        + scan_sems
        + scan_sems
    )
    hbm = pl.BlockSpec(memory_space=pltpu.HBM)
    fa, e = pl.pallas_call(
        functools.partial(kernel, n, m, off),
        out_shape=(
            jax.ShapeDtypeStruct((nd, rows, cols), f32),
            jax.ShapeDtypeStruct((rows, cols), f32),
        ),
        in_specs=[hbm, hbm, hbm, hbm],
        out_specs=(
            pl.BlockSpec(memory_space=pltpu.VMEM),
            pl.BlockSpec(memory_space=pltpu.VMEM),
        ),
        scratch_shapes=scratch,
        compiler_params=pltpu.CompilerParams(
            collective_id=0, has_side_effects=True, vmem_limit_bytes=53_500_000
        ),
        name="render_grad",
    )(light_dir, colour_tint, cotangent, density)
    return fa - e[None]


def solution(mesh):
    placed = (P("ray", "row", None), P(), P(), P(None, "row", None))
    return jax.shard_map(
        functools.partial(local, mesh.shape["ray"], mesh.shape["row"]),
        mesh=mesh,
        in_specs=placed,
        out_specs=P("ray", "row", None),
        check_vma=False,
    )
```
